128 devices in a mesh: pt: 8 (over z, core), comp: 16 (over x, y).
Axes of the slice: x: 4, y: 4, z: 4, core: 2. Of those that a mesh axis runs over, the one named last changes fastest.
Arguments:
- spectrum: float32 [512, 131072], P(None, ('pt', 'comp')), may hold values from 0.1 to 2
- wind: float32 [131072], P(('pt', 'comp')), may hold values from 0.5 to 4
- growth: float32 [512], replicated, may hold values from 0.05 to 0.5
- whitecap: float32 [512], replicated, may hold values from 0.1 to 1
- courant: float32 [16], replicated, may hold values from 0.2 to 0.7
- substeps: int32 [512], replicated, may hold values from 1 to 8, as said below
- limiter: int32 [131072], P(('pt', 'comp')), may hold values 0 or 1
- deck: int32 [131072], replicated, may hold values from 0 to 131071, as said below
- wet: int32 [256, 512], replicated, may hold values 0 or 1
Outputs:
- spectrum_out: float32 [512, 131072], P(None, ('pt', 'comp'))
- height: float32 [131072], P(('pt', 'comp'))
The draws below stay inside these ranges and needn't reach their ends.
Inputs may be any that keep to these rules, and one draw needn't show every extreme that they name: Every component has 1 to 8 substeps, and some component has exactly 8. Each grid cell appears at exactly one deck slot. The deck is dealt in aligned runs of 128 slots: slots k * 128 .. k * 128 + 127 hold 128 consecutive cells, in order, starting at a multiple of 128.
All inputs are finite; a program needn't handle non-finite values. No bound on the sum of `limiter` on one device may be relied on, other than what follows from the above.
Results may differ from the reference program's by a relative error of at most 0.0003.
Values sent between devices are 32-bit elements; how exact they have to be, the bound alone decides.
A program may use at most 64 MiB of HBM per device.

```python
import math
import jax
import jax.numpy as jnp
from jax import lax

DIRS = 32
FREQ = 16
GX = 256
GY = 512
MAXSUB = 8
RUN = 128
COMP = 512
NPTS = 131072


def draw_substeps(key, part):
    counts = jax.random.randint(key, (COMP,), 1, MAXSUB + 1)
    chosen = jax.random.randint(jax.random.fold_in(key, 7), (), 0, COMP)
    return counts.at[chosen].set(MAXSUB).astype(jnp.int32)


def draw_deck(key, part):
    run_count = NPTS // RUN
    shuffled = jax.random.permutation(jax.random.fold_in(key, 11), run_count).astype(jnp.int32)
    offsets = jnp.arange(RUN, dtype=jnp.int32)
    return (shuffled[:, None] * RUN + offsets[None, :]).reshape(NPTS).astype(jnp.int32)


def place_ends(drawn, key, low, largest):
    shape = drawn.shape
    spot = [jax.random.randint(jax.random.fold_in(key, axis), (), 0, shape[axis]) for axis in range(len(shape))]
    drawn = drawn.at[tuple(spot)].set(low)
    longest = shape.index(max(shape))
    spot[longest] = (spot[longest] + 1) % shape[longest]
    return drawn.at[tuple(spot)].set(largest)


def level_of(stream_key, dims, cuts, smallest, largest):
    gain, own = 1.0, jax.random.fold_in(stream_key, 6)
    for dim, blocks in cuts:
        draws = jnp.exp(jax.random.uniform(jax.random.fold_in(own, dim), (blocks,), jnp.float32, smallest / len(cuts), largest / len(cuts)))
        gain = gain * jnp.repeat(draws, dims[dim] // blocks).reshape([-1 if axis == dim else 1 for axis in range(len(dims))])
    return gain


def setup_inputs(seed: int = 0) -> dict:
    seeds = jax.random.split(jax.random.key(seed), 10)
    return {
        "spectrum": jnp.clip(jnp.exp(math.log(2.0) - 2.9957323 * jax.random.uniform(seeds[0], (COMP, NPTS), jnp.float32) ** level_of(seeds[0], (COMP, NPTS), ((1, 128),), -0.2, 0.2)), 0.1, 2.0),
        "wind": jnp.clip(jnp.exp(math.log(4.0) - 2.0794415 * jax.random.uniform(seeds[1], (NPTS,), jnp.float32) ** level_of(seeds[1], (NPTS,), ((0, 128),), -0.2, 0.2)), 0.5, 4.0),
        "growth": jnp.clip(jnp.exp(jax.random.uniform(seeds[2], (COMP,), jnp.float32, math.log(0.05), math.log(0.5))), 0.05, 0.5),
        "whitecap": jnp.clip(jnp.exp(jax.random.uniform(seeds[3], (COMP,), jnp.float32, math.log(0.1), math.log(1.0))), 0.1, 1.0),
        "courant": jnp.clip(jnp.exp(jax.random.uniform(seeds[4], (FREQ,), jnp.float32, math.log(0.2), math.log(0.7))), 0.2, 0.7),
        "substeps": draw_substeps(jax.random.fold_in(seeds[9], 71), 0),
        "limiter": place_ends((jax.random.randint(seeds[6], (NPTS,), 0, 3) < 1).astype(jnp.int32), jax.random.fold_in(seeds[6], 1), 0, 1),
        "deck": draw_deck(jax.random.fold_in(seeds[9], 71), 0),
        "wet": place_ends((jax.random.randint(seeds[8], (GX, GY), 0, 4) < 3).astype(jnp.int32), jax.random.fold_in(seeds[8], 1), 0, 1),
    }


rate_limit = 0.5
time_step = 0.5

def sources(spectrum, wind, growth, whitecap, limiter):
    mean_energy = lax.optimization_barrier(jnp.mean(spectrum, axis=0))
    rate = wind[None, :] * growth[:, None] - whitecap[:, None] * (mean_energy / (1.0 + mean_energy))[None, :]
    rate = jnp.where(limiter[None, :] == 1, rate_limit * jnp.tanh(rate / rate_limit), rate)
    return spectrum * jnp.exp(time_step * rate)

def substep(field_grid, cross, along, wetness):
    sea = field_grid * wetness[None, :, :]
    east = jnp.roll(sea, 1, axis=2)
    west = jnp.roll(sea, -1, axis=2)
    up_column = jnp.where(along[:, None, None] > 0, east, west)
    zero_row = jnp.zeros_like(sea[:, :1, :])
    south = jnp.concatenate([zero_row, sea[:, :-1, :]], axis=1)
    north = jnp.concatenate([sea[:, 1:, :], zero_row], axis=1)
    up_row = jnp.where(cross[:, None, None] > 0, south, north)
    moved = field_grid - jnp.abs(cross)[:, None, None] * (field_grid - up_row) - jnp.abs(along)[:, None, None] * (field_grid - up_column)
    return jnp.where(wetness[None, :, :] > 0, moved, field_grid)

def reference(spectrum, wind, growth, whitecap, courant, substeps, limiter, deck, wet):
    forced = sources(spectrum, wind, growth, whitecap, limiter)
    inverse = jnp.zeros((NPTS,), jnp.int32).at[deck].set(jnp.arange(NPTS, dtype=jnp.int32))
    wetness = wet.astype(jnp.float32)
    comps = jnp.arange(COMP, dtype=jnp.int32)
    angle = 2.0 * math.pi / DIRS * ((comps % DIRS).astype(jnp.float32) + 0.5)
    speed = courant[comps // DIRS]
    cross = speed * jnp.sin(angle)
    along = speed * jnp.cos(angle)

    def block(items):
        fields, cr, al, counts = items
        field_grid = fields[:, inverse].reshape(-1, GX, GY)
        for step in range(MAXSUB):
            field_grid = jnp.where(step < counts[:, None, None], substep(field_grid, cr, al, wetness), field_grid)
        return field_grid.reshape(-1, NPTS)[:, deck]
    blocks = COMP // 16
    result = lax.map(block, (forced.reshape(blocks, 16, NPTS), cross.reshape(blocks, 16), along.reshape(blocks, 16), substeps.reshape(blocks, 16)))
    spectrum_out = result.reshape(COMP, NPTS)
    height = 4.0 * jnp.sqrt(lax.optimization_barrier(jnp.mean(spectrum_out, axis=0)) + 1e-06)
    return (spectrum_out, height)
```

```python
import functools
import math

import jax
import jax.numpy as jnp
from jax import lax
from jax.experimental import pallas as pl
from jax.experimental.pallas import tpu as pltpu
from jax.sharding import PartitionSpec as P

DIRS = 32
MAXSUB = 8
RUN = 128
SUB = 8


rate_limit = 0.5
time_step = 0.5


def sources(spectrum, wind, growth, whitecap, limiter):
    mean_energy = jnp.mean(spectrum, axis=0)
    rate = (
        wind[None, :] * growth[:, None]
        - whitecap[:, None] * (mean_energy / (1.0 + mean_energy))[None, :]
    )
    rate = jnp.where(limiter[None, :] == 1, rate_limit * jnp.tanh(rate / rate_limit), rate)
    return spectrum * jnp.exp(time_step * rate)


def propagate_kernel(inv_ref, ax_ref, ay_ref, var_ref, cnt_ref, recv_ref, wet_ref, out_ref, buf_ref):
    comps = recv_ref.shape[0]
    slabs = wet_ref.shape[0]
    cols = wet_ref.shape[2]
    quarters = cols // RUN

    def copy_runs(c, to_grid, slot):
        def body(j, carry):
            for k in range(SUB):
                for q in range(quarters):
                    s = inv_ref[(k * slabs + j) * quarters + q]
                    lanes = slice(q * RUN, (q + 1) * RUN)
                    if to_grid:
                        buf_ref[slot, j, k:k + 1, lanes] = recv_ref[c, pl.ds(s, 1), :]
                    else:
                        out_ref[c, pl.ds(s, 1), :] = buf_ref[slot, j, k:k + 1, lanes]
            return carry

        lax.fori_loop(0, slabs, body, 0)

    def substep(src, dst, south, east, axc, ayc):
        sub_id = lax.broadcasted_iota(jnp.int32, (SUB, cols), 0)
        if south:
            edge = buf_ref[src, slabs - 1] * wet_ref[slabs - 1]
            init = jnp.where(sub_id == 0, 0.0, pltpu.roll(edge, 1, 0))
        else:
            edge = buf_ref[src, 0] * wet_ref[0]
            init = jnp.where(sub_id == SUB - 1, 0.0, pltpu.roll(edge, SUB - 1, 0))

        def body(i, up_row):
            j = i if south else slabs - 1 - i
            f = buf_ref[src, j]
            w = wet_ref[j]
            sea = f * w
            up_col = pltpu.roll(sea, 1 if east else cols - 1, 1)
            moved = f - axc * (f - up_row) - ayc * (f - up_col)
            buf_ref[dst, j] = jnp.where(w > 0, moved, f)
            return sea

        lax.fori_loop(0, slabs, body, init, unroll=2)

    def variant(south, east, c):
        axc = ax_ref[c]
        ayc = ay_ref[c]
        cnt = cnt_ref[c]
        for n in range(MAXSUB):
            @pl.when(n < cnt)
            def _():
                substep(n % 2, (n + 1) % 2, south, east, axc, ayc)

    def comp_body(c, carry):
        copy_runs(c, True, 0)
        v = var_ref[c]
        for vi, (south, east) in enumerate(((False, False), (False, True), (True, False), (True, True))):
            @pl.when(v == vi)
            def _():
                variant(south, east, c)
        fin = cnt_ref[c] % 2
        copy_runs_dyn(c, fin)
        return carry

    def copy_runs_dyn(c, slot):
        def body(j, carry):
            for k in range(SUB):
                for q in range(quarters):
                    s = inv_ref[(k * slabs + j) * quarters + q]
                    out_ref[c, pl.ds(s, 1), :] = buf_ref[slot, j, k:k + 1, q * RUN:(q + 1) * RUN]
            return carry

        lax.fori_loop(0, slabs, body, 0)

    lax.fori_loop(0, comps, comp_body, 0)


def propagate(inv, ax, ay, var, cnt, recv, wet_t):
    comps, nruns, _ = recv.shape
    slabs, _, cols = wet_t.shape
    smem = pl.BlockSpec(memory_space=pltpu.SMEM)
    vmem = pl.BlockSpec(memory_space=pltpu.VMEM)
    return pl.pallas_call(
        propagate_kernel,
        out_shape=jax.ShapeDtypeStruct(recv.shape, recv.dtype),
        in_specs=[smem] * 5 + [vmem] * 2,
        out_specs=vmem,
        scratch_shapes=[pltpu.VMEM((2, slabs, SUB, cols), jnp.float32)],
    )(inv, ax, ay, var, cnt, recv, wet_t)


def on_device(spectrum, wind, growth, whitecap, courant, substeps, limiter, deck, wet):
    forced = sources(spectrum, wind, growth, whitecap, limiter)
    pt_count = lax.axis_size("pt")
    comp_count = lax.axis_size("comp")
    group_size = pt_count * comp_count
    total_comps = forced.shape[0]
    point_count = forced.shape[1]
    per_device = total_comps // group_size
    all_points = deck.shape[0]
    rows_grid = wet.shape[0]
    cols_grid = wet.shape[1]
    run_count = all_points // RUN
    received = lax.all_to_all(
        forced.reshape(per_device, group_size, point_count),
        ("pt", "comp"),
        split_axis=1,
        concat_axis=1,
        tiled=True,
    )
    fields = received.reshape(per_device, run_count, RUN)
    own_rank = lax.axis_index("pt") * comp_count + lax.axis_index("comp")
    comps = jnp.arange(per_device, dtype=jnp.int32) * group_size + own_rank
    angle = 2.0 * math.pi / DIRS * ((comps % DIRS).astype(jnp.float32) + 0.5)
    speed = courant[comps // DIRS]
    cross = speed * jnp.sin(angle)
    along = speed * jnp.cos(angle)
    counts = substeps[comps]
    var = (cross > 0).astype(jnp.int32) * 2 + (along > 0).astype(jnp.int32)
    slabs = rows_grid // SUB
    wet_t = wet.astype(jnp.float32).reshape(SUB, slabs, cols_grid).transpose(1, 0, 2)
    slot_runs = deck.reshape(run_count, RUN)[:, 0] // RUN
    inv = jnp.zeros((run_count,), jnp.int32).at[slot_runs].set(jnp.arange(run_count, dtype=jnp.int32))
    slots = propagate(inv, jnp.abs(cross), jnp.abs(along), var, counts, fields, wet_t)
    back = lax.all_to_all(
        slots.reshape(per_device, group_size, point_count),
        ("pt", "comp"),
        split_axis=1,
        concat_axis=1,
        tiled=True,
    )
    arrived = back.reshape(total_comps, point_count)
    height = 4.0 * jnp.sqrt(jnp.mean(arrived, axis=0) + 1e-06)
    return (arrived, height)


def solution(mesh):
    in_specs = (
        P(None, ("pt", "comp")),
        P(("pt", "comp")),
        P(),
        P(),
        P(),
        P(),
        P(("pt", "comp")),
        P(),
        P(),
    )
    out_specs = (P(None, ("pt", "comp")), P(("pt", "comp")))
    return jax.shard_map(
        on_device, mesh=mesh, in_specs=in_specs, out_specs=out_specs, check_vma=False
    )
```

```python
import functools
import math

import jax
import jax.numpy as jnp
from jax import lax
from jax.experimental import pallas as pl
from jax.experimental.pallas import tpu as pltpu
from jax.sharding import PartitionSpec as P

DIRS = 32
MAXSUB = 8
RUN = 128
SUB = 8


rate_limit = 0.5
time_step = 0.5


def sources(spectrum, wind, growth, whitecap, limiter):
    mean_energy = jnp.mean(spectrum, axis=0)
    rate = (
        wind[None, :] * growth[:, None]
        - whitecap[:, None] * (mean_energy / (1.0 + mean_energy))[None, :]
    )
    rate = jnp.where(limiter[None, :] == 1, rate_limit * jnp.tanh(rate / rate_limit), rate)
    return spectrum * jnp.exp(time_step * rate)


def propagate_kernel(inv_ref, ax_ref, ay_ref, var_ref, cnt_ref, recv_ref, wet_ref, out_ref, buf_ref):
    comps = recv_ref.shape[0]
    slabs = wet_ref.shape[0]
    cols = wet_ref.shape[2]
    quarters = cols // RUN

    def copy_runs(c, to_grid, slot):
        def body(j, carry):
            for k in range(SUB):
                for q in range(quarters):
                    s = inv_ref[(k * slabs + j) * quarters + q]
                    lanes = slice(q * RUN, (q + 1) * RUN)
                    if to_grid:
                        buf_ref[slot, j, k:k + 1, lanes] = recv_ref[c, pl.ds(s, 1), :]
                    else:
                        out_ref[c, pl.ds(s, 1), :] = buf_ref[slot, j, k:k + 1, lanes]
            return carry

        lax.fori_loop(0, slabs, body, 0)

    def substep(src, dst, south, east, axc, ayc):
        sub_id = lax.broadcasted_iota(jnp.int32, (SUB, cols), 0)
        if south:
            edge = buf_ref[src, slabs - 1] * wet_ref[slabs - 1]
            init = jnp.where(sub_id == 0, 0.0, pltpu.roll(edge, 1, 0))
        else:
            edge = buf_ref[src, 0] * wet_ref[0]
            init = jnp.where(sub_id == SUB - 1, 0.0, pltpu.roll(edge, SUB - 1, 0))

        def body(i, up_row):
            j = i if south else slabs - 1 - i
            f = buf_ref[src, j]
            w = wet_ref[j]
            sea = f * w
            up_col = pltpu.roll(sea, 1 if east else cols - 1, 1)
            moved = f - axc * (f - up_row) - ayc * (f - up_col)
            buf_ref[dst, j] = jnp.where(w > 0, moved, f)
            return sea

        lax.fori_loop(0, slabs, body, init, unroll=True)

    def variant(south, east, c):
        axc = ax_ref[c]
        ayc = ay_ref[c]
        cnt = cnt_ref[c]
        for n in range(MAXSUB):
            @pl.when(n < cnt)
            def _():
                substep(n % 2, (n + 1) % 2, south, east, axc, ayc)

    def comp_body(c, carry):
        copy_runs(c, True, 0)
        v = var_ref[c]
        for vi, (south, east) in enumerate(((False, False), (False, True), (True, False), (True, True))):
            @pl.when(v == vi)
            def _():
                variant(south, east, c)
        fin = cnt_ref[c] % 2
        copy_runs_dyn(c, fin)
        return carry

    def copy_runs_dyn(c, slot):
        def body(j, carry):
            for k in range(SUB):
                for q in range(quarters):
                    s = inv_ref[(k * slabs + j) * quarters + q]
                    out_ref[c, pl.ds(s, 1), :] = buf_ref[slot, j, k:k + 1, q * RUN:(q + 1) * RUN]
            return carry

        lax.fori_loop(0, slabs, body, 0)

    lax.fori_loop(0, comps, comp_body, 0)


def propagate(inv, ax, ay, var, cnt, recv, wet_t):
    comps, nruns, _ = recv.shape
    slabs, _, cols = wet_t.shape
    smem = pl.BlockSpec(memory_space=pltpu.SMEM)
    vmem = pl.BlockSpec(memory_space=pltpu.VMEM)
    return pl.pallas_call(
        propagate_kernel,
        out_shape=jax.ShapeDtypeStruct(recv.shape, recv.dtype),
        in_specs=[smem] * 5 + [vmem] * 2,
        out_specs=vmem,
        scratch_shapes=[pltpu.VMEM((2, slabs, SUB, cols), jnp.float32)],
    )(inv, ax, ay, var, cnt, recv, wet_t)


def on_device(spectrum, wind, growth, whitecap, courant, substeps, limiter, deck, wet):
    forced = sources(spectrum, wind, growth, whitecap, limiter)
    pt_count = lax.axis_size("pt")
    comp_count = lax.axis_size("comp")
    group_size = pt_count * comp_count
    total_comps = forced.shape[0]
    point_count = forced.shape[1]
    per_device = total_comps // group_size
    all_points = deck.shape[0]
    rows_grid = wet.shape[0]
    cols_grid = wet.shape[1]
    run_count = all_points // RUN
    received = lax.all_to_all(
        forced.reshape(per_device, group_size, point_count),
        ("pt", "comp"),
        split_axis=1,
        concat_axis=1,
        tiled=True,
    )
    fields = received.reshape(per_device, run_count, RUN)
    own_rank = lax.axis_index("pt") * comp_count + lax.axis_index("comp")
    comps = jnp.arange(per_device, dtype=jnp.int32) * group_size + own_rank
    angle = 2.0 * math.pi / DIRS * ((comps % DIRS).astype(jnp.float32) + 0.5)
    speed = courant[comps // DIRS]
    cross = speed * jnp.sin(angle)
    along = speed * jnp.cos(angle)
    counts = substeps[comps]
    var = (cross > 0).astype(jnp.int32) * 2 + (along > 0).astype(jnp.int32)
    slabs = rows_grid // SUB
    wet_t = wet.astype(jnp.float32).reshape(SUB, slabs, cols_grid).transpose(1, 0, 2)
    slot_runs = deck.reshape(run_count, RUN)[:, 0] // RUN
    inv = jnp.zeros((run_count,), jnp.int32).at[slot_runs].set(jnp.arange(run_count, dtype=jnp.int32))
    slots = propagate(inv, jnp.abs(cross), jnp.abs(along), var, counts, fields, wet_t)
    back = lax.all_to_all(
        slots.reshape(per_device, group_size, point_count),
        ("pt", "comp"),
        split_axis=1,
        concat_axis=1,
        tiled=True,
    )
    arrived = back.reshape(total_comps, point_count)
    height = 4.0 * jnp.sqrt(jnp.mean(arrived, axis=0) + 1e-06)
    return (arrived, height)


def solution(mesh):
    in_specs = (
        P(None, ("pt", "comp")),
        P(("pt", "comp")),
        P(),
        P(),
        P(),
        P(),
        P(("pt", "comp")),
        P(),
        P(),
    )
    out_specs = (P(None, ("pt", "comp")), P(("pt", "comp")))
    return jax.shard_map(
        on_device, mesh=mesh, in_specs=in_specs, out_specs=out_specs, check_vma=False
    )
```

```python
import functools
import math

import jax
import jax.numpy as jnp
from jax import lax
from jax.experimental import pallas as pl
from jax.experimental.pallas import tpu as pltpu
from jax.sharding import PartitionSpec as P

DIRS = 32
MAXSUB = 8
RUN = 128
SUB = 8


rate_limit = 0.5
time_step = 0.5


def sources(spectrum, wind, growth, whitecap, limiter):
    mean_energy = jnp.mean(spectrum, axis=0)
    rate = (
        wind[None, :] * growth[:, None]
        - whitecap[:, None] * (mean_energy / (1.0 + mean_energy))[None, :]
    )
    rate = jnp.where(limiter[None, :] == 1, rate_limit * jnp.tanh(rate / rate_limit), rate)
    return spectrum * jnp.exp(time_step * rate)


def propagate_kernel(inv_ref, ax_ref, ay_ref, var_ref, cnt_ref, recv_ref, wet_ref, out_ref, buf_ref):
    comps = recv_ref.shape[1]
    runs_per_dev = recv_ref.shape[2] // RUN
    slabs = wet_ref.shape[0]
    cols = wet_ref.shape[2]
    quarters = cols // RUN

    def copy_runs(c, to_grid):
        slot = 0 if to_grid else cnt_ref[c] % 2

        def body(j, carry):
            for k in range(SUB):
                for q in range(quarters):
                    s = inv_ref[(k * slabs + j) * quarters + q]
                    src = s // runs_per_dev
                    off = pl.multiple_of((s % runs_per_dev) * RUN, RUN)
                    lanes = slice(q * RUN, (q + 1) * RUN)
                    if to_grid:
                        buf_ref[c, slot, j, k:k + 1, lanes] = recv_ref[src, c:c + 1, pl.ds(off, RUN)]
                    else:
                        out_ref[src, c:c + 1, pl.ds(off, RUN)] = buf_ref[c, slot, j, k:k + 1, lanes]
            return carry

        lax.fori_loop(0, slabs, body, 0)

    def substep(c, src, dst, south, east, axc, ayc):
        sub_id = lax.broadcasted_iota(jnp.int32, (SUB, cols), 0)
        if south:
            edge = buf_ref[c, src, slabs - 1] * wet_ref[slabs - 1]
            init = jnp.where(sub_id == 0, 0.0, pltpu.roll(edge, 1, 0))
        else:
            edge = buf_ref[c, src, 0] * wet_ref[0]
            init = jnp.where(sub_id == SUB - 1, 0.0, pltpu.roll(edge, SUB - 1, 0))

        def body(i, up_row):
            j = i if south else slabs - 1 - i
            f = buf_ref[c, src, j]
            w = wet_ref[j]
            sea = f * w
            up_col = pltpu.roll(sea, 1 if east else cols - 1, 1)
            moved = f - axc * (f - up_row) - ayc * (f - up_col)
            buf_ref[c, dst, j] = jnp.where(w > 0, moved, f)
            return sea

        lax.fori_loop(0, slabs, body, init, unroll=True)

    def variant(south, east, c):
        axc = ax_ref[c]
        ayc = ay_ref[c]
        cnt = cnt_ref[c]
        for n in range(MAXSUB):
            @pl.when(n < cnt)
            def _():
                substep(c, n % 2, (n + 1) % 2, south, east, axc, ayc)

    def comp_body(c, carry):
        v = var_ref[c]
        for vi, (south, east) in enumerate(((False, False), (False, True), (True, False), (True, True))):
            @pl.when(v == vi)
            def _():
                variant(south, east, c)
        return carry

    for c in range(comps):
        copy_runs(c, True)
    lax.fori_loop(0, comps, comp_body, 0)
    for c in range(comps):
        copy_runs(c, False)


def propagate(inv, ax, ay, var, cnt, recv, wet_t):
    slabs, _, cols = wet_t.shape
    smem = pl.BlockSpec(memory_space=pltpu.SMEM)
    vmem = pl.BlockSpec(memory_space=pltpu.VMEM)
    return pl.pallas_call(
        propagate_kernel,
        out_shape=jax.ShapeDtypeStruct(recv.shape, recv.dtype),
        in_specs=[smem] * 5 + [vmem] * 2,
        out_specs=vmem,
        scratch_shapes=[pltpu.VMEM((recv.shape[1], 2, slabs, SUB, cols), jnp.float32)],
    )(inv, ax, ay, var, cnt, recv, wet_t)


def on_device(spectrum, wind, growth, whitecap, courant, substeps, limiter, deck, wet):
    forced = sources(spectrum, wind, growth, whitecap, limiter)
    pt_count = lax.axis_size("pt")
    comp_count = lax.axis_size("comp")
    group_size = pt_count * comp_count
    total_comps = forced.shape[0]
    point_count = forced.shape[1]
    per_device = total_comps // group_size
    all_points = deck.shape[0]
    rows_grid = wet.shape[0]
    cols_grid = wet.shape[1]
    run_count = all_points // RUN
    fields = lax.all_to_all(
        forced.reshape(group_size, per_device, point_count),
        ("pt", "comp"),
        split_axis=0,
        concat_axis=0,
        tiled=True,
    )
    own_rank = lax.axis_index("pt") * comp_count + lax.axis_index("comp")
    comps = own_rank * per_device + jnp.arange(per_device, dtype=jnp.int32)
    angle = 2.0 * math.pi / DIRS * ((comps % DIRS).astype(jnp.float32) + 0.5)
    speed = courant[comps // DIRS]
    cross = speed * jnp.sin(angle)
    along = speed * jnp.cos(angle)
    counts = substeps[comps]
    var = (cross > 0).astype(jnp.int32) * 2 + (along > 0).astype(jnp.int32)
    slabs = rows_grid // SUB
    wet_t = wet.astype(jnp.float32).reshape(SUB, slabs, cols_grid).transpose(1, 0, 2)
    slot_runs = deck.reshape(run_count, RUN)[:, 0] // RUN
    run_ids = jnp.arange(run_count, dtype=jnp.int32)
    inv = jnp.sum(jnp.where(slot_runs[None, :] == run_ids[:, None], run_ids[None, :], 0), axis=1)
    slots = propagate(inv, jnp.abs(cross), jnp.abs(along), var, counts, fields, wet_t)
    back = lax.all_to_all(slots, ("pt", "comp"), split_axis=0, concat_axis=0, tiled=True)
    arrived = back.reshape(total_comps, point_count)
    height = 4.0 * jnp.sqrt(jnp.mean(arrived, axis=0) + 1e-06)
    return (arrived, height)


def solution(mesh):
    in_specs = (
        P(None, ("pt", "comp")),
        P(("pt", "comp")),
        P(),
        P(),
        P(),
        P(),
        P(("pt", "comp")),
        P(),
        P(),
    )
    out_specs = (P(None, ("pt", "comp")), P(("pt", "comp")))
    return jax.shard_map(
        on_device, mesh=mesh, in_specs=in_specs, out_specs=out_specs, check_vma=False
    )
```

```python
import functools
import math

import jax
import jax.numpy as jnp
from jax import lax
from jax.experimental import pallas as pl
from jax.experimental.pallas import tpu as pltpu
from jax.sharding import PartitionSpec as P

DIRS = 32
MAXSUB = 8
RUN = 128
SUB = 8


rate_limit = 0.5
time_step = 0.5


def sources(spectrum, wind, growth, whitecap, limiter):
    mean_energy = jnp.mean(spectrum, axis=0)
    rate = (
        wind[None, :] * growth[:, None]
        - whitecap[:, None] * (mean_energy / (1.0 + mean_energy))[None, :]
    )
    rate = jnp.where(limiter[None, :] == 1, rate_limit * jnp.tanh(rate / rate_limit), rate)
    return spectrum * jnp.exp(time_step * rate)


def propagate_kernel(inv_ref, ax_ref, ay_ref, var_ref, cnt_ref, recv_ref, wet_ref, out_ref, buf_ref):
    comps = recv_ref.shape[2]
    runs_per_dev = recv_ref.shape[1]
    slabs = wet_ref.shape[0]
    cols = wet_ref.shape[2]
    quarters = cols // RUN

    def copy_runs(c, to_grid):
        slot = 0 if to_grid else cnt_ref[c] % 2

        def body(j, carry):
            for k in range(SUB):
                for q in range(quarters):
                    s = inv_ref[(k * slabs + j) * quarters + q]
                    src = s // runs_per_dev
                    m = s % runs_per_dev
                    lanes = slice(q * RUN, (q + 1) * RUN)
                    if to_grid:
                        buf_ref[c, slot, j, k:k + 1, lanes] = recv_ref[src, m, c:c + 1, :]
                    else:
                        out_ref[src, m, c:c + 1, :] = buf_ref[c, slot, j, k:k + 1, lanes]
            return carry

        lax.fori_loop(0, slabs, body, 0)

    def substep(c, src, dst, south, east, axc, ayc):
        sub_id = lax.broadcasted_iota(jnp.int32, (SUB, cols), 0)
        if south:
            edge = buf_ref[c, src, slabs - 1] * wet_ref[slabs - 1]
            init = jnp.where(sub_id == 0, 0.0, pltpu.roll(edge, 1, 0))
        else:
            edge = buf_ref[c, src, 0] * wet_ref[0]
            init = jnp.where(sub_id == SUB - 1, 0.0, pltpu.roll(edge, SUB - 1, 0))

        def body(i, up_row):
            j = i if south else slabs - 1 - i
            f = buf_ref[c, src, j]
            w = wet_ref[j]
            sea = f * w
            up_col = pltpu.roll(sea, 1 if east else cols - 1, 1)
            moved = f - axc * (f - up_row) - ayc * (f - up_col)
            buf_ref[c, dst, j] = jnp.where(w > 0, moved, f)
            return sea

        lax.fori_loop(0, slabs, body, init, unroll=True)

    def variant(south, east, c):
        axc = ax_ref[c]
        ayc = ay_ref[c]
        cnt = cnt_ref[c]
        for n in range(MAXSUB):
            @pl.when(n < cnt)
            def _():
                substep(c, n % 2, (n + 1) % 2, south, east, axc, ayc)

    def comp_body(c, carry):
        v = var_ref[c]
        for vi, (south, east) in enumerate(((False, False), (False, True), (True, False), (True, True))):
            @pl.when(v == vi)
            def _():
                variant(south, east, c)
        return carry

    for c in range(comps):
        copy_runs(c, True)
    lax.fori_loop(0, comps, comp_body, 0)
    for c in range(comps):
        copy_runs(c, False)


def propagate(inv, ax, ay, var, cnt, recv, wet_t):
    slabs, _, cols = wet_t.shape
    smem = pl.BlockSpec(memory_space=pltpu.SMEM)
    vmem = pl.BlockSpec(memory_space=pltpu.VMEM)
    return pl.pallas_call(
        propagate_kernel,
        out_shape=jax.ShapeDtypeStruct(recv.shape, recv.dtype),
        in_specs=[smem] * 5 + [vmem] * 2,
        out_specs=vmem,
        scratch_shapes=[pltpu.VMEM((recv.shape[2], 2, slabs, SUB, cols), jnp.float32)],
    )(inv, ax, ay, var, cnt, recv, wet_t)


def on_device(spectrum, wind, growth, whitecap, courant, substeps, limiter, deck, wet):
    forced = sources(spectrum, wind, growth, whitecap, limiter)
    pt_count = lax.axis_size("pt")
    comp_count = lax.axis_size("comp")
    group_size = pt_count * comp_count
    total_comps = forced.shape[0]
    point_count = forced.shape[1]
    per_device = total_comps // group_size
    all_points = deck.shape[0]
    rows_grid = wet.shape[0]
    cols_grid = wet.shape[1]
    run_count = all_points // RUN
    runs_per_dev = point_count // RUN
    fields = lax.all_to_all(
        forced.reshape(group_size, per_device, runs_per_dev, RUN).transpose(0, 2, 1, 3),
        ("pt", "comp"),
        split_axis=0,
        concat_axis=0,
        tiled=True,
    )
    own_rank = lax.axis_index("pt") * comp_count + lax.axis_index("comp")
    comps = own_rank * per_device + jnp.arange(per_device, dtype=jnp.int32)
    angle = 2.0 * math.pi / DIRS * ((comps % DIRS).astype(jnp.float32) + 0.5)
    speed = courant[comps // DIRS]
    cross = speed * jnp.sin(angle)
    along = speed * jnp.cos(angle)
    counts = substeps[comps]
    var = (cross > 0).astype(jnp.int32) * 2 + (along > 0).astype(jnp.int32)
    slabs = rows_grid // SUB
    wet_t = wet.astype(jnp.float32).reshape(SUB, slabs, cols_grid).transpose(1, 0, 2)
    slot_runs = deck.reshape(run_count, RUN)[:, 0] // RUN
    run_ids = jnp.arange(run_count, dtype=jnp.int32)
    inv = jnp.sum(jnp.where(slot_runs[None, :] == run_ids[:, None], run_ids[None, :], 0), axis=1)
    slots = propagate(inv, jnp.abs(cross), jnp.abs(along), var, counts, fields, wet_t)
    back = lax.all_to_all(slots, ("pt", "comp"), split_axis=0, concat_axis=0, tiled=True)
    arrived = back.transpose(0, 2, 1, 3).reshape(total_comps, point_count)
    height = 4.0 * jnp.sqrt(jnp.mean(arrived, axis=0) + 1e-06)
    return (arrived, height)


def solution(mesh):
    in_specs = (
        P(None, ("pt", "comp")),
        P(("pt", "comp")),
        P(),
        P(),
        P(),
        P(),
        P(("pt", "comp")),
        P(),
        P(),
    )
    out_specs = (P(None, ("pt", "comp")), P(("pt", "comp")))
    return jax.shard_map(
        on_device, mesh=mesh, in_specs=in_specs, out_specs=out_specs, check_vma=False
    )
```

```python
import functools
import math

import jax
import jax.numpy as jnp
from jax import lax
from jax.experimental import pallas as pl
from jax.experimental.pallas import tpu as pltpu
from jax.sharding import PartitionSpec as P

DIRS = 32
MAXSUB = 8
RUN = 128
SUB = 8


rate_limit = 0.5
time_step = 0.5


def sources(spectrum, wind, growth, whitecap, limiter):
    mean_energy = jnp.mean(spectrum, axis=0)
    rate = (
        wind[None, :] * growth[:, None]
        - whitecap[:, None] * (mean_energy / (1.0 + mean_energy))[None, :]
    )
    rate = jnp.where(limiter[None, :] == 1, rate_limit * jnp.tanh(rate / rate_limit), rate)
    return spectrum * jnp.exp(time_step * rate)


def propagate_kernel(inv_ref, ax_ref, ay_ref, var_ref, cnt_ref, recv_ref, wet_ref, out_ref, buf_ref):
    comps = recv_ref.shape[2]
    runs_per_dev = recv_ref.shape[1]
    slabs = wet_ref.shape[0]
    cols = wet_ref.shape[2]
    quarters = cols // RUN

    def copy_runs(c, to_grid):
        slot = 0 if to_grid else cnt_ref[c] % 2
        buf_c = buf_ref

        def body(j, carry):
            for k in range(SUB):
                for q in range(quarters):
                    s = inv_ref[(k * slabs + j) * quarters + q]
                    src = s // runs_per_dev
                    m = s % runs_per_dev
                    lanes = slice(q * RUN, (q + 1) * RUN)
                    if to_grid:
                        buf_c[slot, j, k:k + 1, lanes] = recv_ref[src, m, c:c + 1, :]
                    else:
                        out_ref[src, m, c:c + 1, :] = buf_c[slot, j, k:k + 1, lanes]
            return carry

        lax.fori_loop(0, slabs, body, 0)

    def substep(c, src, dst, south, east, axc, ayc):
        sub_id = lax.broadcasted_iota(jnp.int32, (SUB, cols), 0)
        if south:
            edge = buf_ref[src, slabs - 1] * wet_ref[slabs - 1]
            init = jnp.where(sub_id == 0, 0.0, pltpu.roll(edge, 1, 0))
        else:
            edge = buf_ref[src, 0] * wet_ref[0]
            init = jnp.where(sub_id == SUB - 1, 0.0, pltpu.roll(edge, SUB - 1, 0))

        def body(i, up_row):
            j = i if south else slabs - 1 - i
            f = buf_ref[src, j]
            w = wet_ref[j]
            sea = f * w
            up_col = pltpu.roll(sea, 1 if east else cols - 1, 1)
            moved = f - axc * (f - up_row) - ayc * (f - up_col)
            buf_ref[dst, j] = jnp.where(w > 0, moved, f)
            return sea

        lax.fori_loop(0, slabs, body, init, unroll=True)

    def variant(south, east, c):
        axc = ax_ref[c]
        ayc = ay_ref[c]
        cnt = cnt_ref[c]
        for n in range(MAXSUB):
            @pl.when(n < cnt)
            def _():
                substep(c, n % 2, (n + 1) % 2, south, east, axc, ayc)

    def comp_body(c, carry):
        for cc in range(comps):
            @pl.when(c == cc)
            def _():
                copy_runs(cc, True)
        v = var_ref[c]
        for vi, (south, east) in enumerate(((False, False), (False, True), (True, False), (True, True))):
            @pl.when(v == vi)
            def _():
                variant(south, east, c)
        for cc in range(comps):
            @pl.when(c == cc)
            def _():
                copy_runs(cc, False)
        return carry

    lax.fori_loop(0, comps, comp_body, 0)


def propagate(inv, ax, ay, var, cnt, recv, wet_t):
    slabs, _, cols = wet_t.shape
    smem = pl.BlockSpec(memory_space=pltpu.SMEM)
    vmem = pl.BlockSpec(memory_space=pltpu.VMEM)
    return pl.pallas_call(
        propagate_kernel,
        out_shape=jax.ShapeDtypeStruct(recv.shape, recv.dtype),
        in_specs=[smem] * 5 + [vmem] * 2,
        out_specs=vmem,
        scratch_shapes=[pltpu.VMEM((2, slabs, SUB, cols), jnp.float32)],
    )(inv, ax, ay, var, cnt, recv, wet_t)


def on_device(spectrum, wind, growth, whitecap, courant, substeps, limiter, deck, wet):
    forced = sources(spectrum, wind, growth, whitecap, limiter)
    pt_count = lax.axis_size("pt")
    comp_count = lax.axis_size("comp")
    group_size = pt_count * comp_count
    total_comps = forced.shape[0]
    point_count = forced.shape[1]
    per_device = total_comps // group_size
    all_points = deck.shape[0]
    rows_grid = wet.shape[0]
    cols_grid = wet.shape[1]
    run_count = all_points // RUN
    runs_per_dev = point_count // RUN
    fields = lax.all_to_all(
        forced.reshape(group_size, per_device, runs_per_dev, RUN).transpose(0, 2, 1, 3),
        ("pt", "comp"),
        split_axis=0,
        concat_axis=0,
        tiled=True,
    )
    own_rank = lax.axis_index("pt") * comp_count + lax.axis_index("comp")
    comps = own_rank * per_device + jnp.arange(per_device, dtype=jnp.int32)
    angle = 2.0 * math.pi / DIRS * ((comps % DIRS).astype(jnp.float32) + 0.5)
    speed = courant[comps // DIRS]
    cross = speed * jnp.sin(angle)
    along = speed * jnp.cos(angle)
    counts = substeps[comps]
    var = (cross > 0).astype(jnp.int32) * 2 + (along > 0).astype(jnp.int32)
    slabs = rows_grid // SUB
    wet_t = wet.astype(jnp.float32).reshape(SUB, slabs, cols_grid).transpose(1, 0, 2)
    slot_runs = deck.reshape(run_count, RUN)[:, 0] // RUN
    run_ids = jnp.arange(run_count, dtype=jnp.int32)
    inv = jnp.sum(jnp.where(slot_runs[None, :] == run_ids[:, None], run_ids[None, :], 0), axis=1)
    slots = propagate(inv, jnp.abs(cross), jnp.abs(along), var, counts, fields, wet_t)
    back = lax.all_to_all(slots, ("pt", "comp"), split_axis=0, concat_axis=0, tiled=True)
    arrived = back.transpose(0, 2, 1, 3).reshape(total_comps, point_count)
    height = 4.0 * jnp.sqrt(jnp.mean(arrived, axis=0) + 1e-06)
    return (arrived, height)


def solution(mesh):
    in_specs = (
        P(None, ("pt", "comp")),
        P(("pt", "comp")),
        P(),
        P(),
        P(),
        P(),
        P(("pt", "comp")),
        P(),
        P(),
    )
    out_specs = (P(None, ("pt", "comp")), P(("pt", "comp")))
    return jax.shard_map(
        on_device, mesh=mesh, in_specs=in_specs, out_specs=out_specs, check_vma=False
    )
```

```python
import functools
import math

import jax
import jax.numpy as jnp
from jax import lax
from jax.experimental import pallas as pl
from jax.experimental.pallas import tpu as pltpu
from jax.sharding import PartitionSpec as P

DIRS = 32
MAXSUB = 8
RUN = 128
SUB = 8


rate_limit = 0.5
time_step = 0.5


def sources(spectrum, wind, growth, whitecap, limiter):
    mean_energy = jnp.mean(spectrum, axis=0)
    rate = (
        wind[None, :] * growth[:, None]
        - whitecap[:, None] * (mean_energy / (1.0 + mean_energy))[None, :]
    )
    rate = jnp.where(limiter[None, :] == 1, rate_limit * jnp.tanh(rate / rate_limit), rate)
    return spectrum * jnp.exp(time_step * rate)


def propagate_kernel(inv_ref, coef_ref, recv_ref, wet_ref, out_ref, buf_ref):
    comps = recv_ref.shape[2]
    runs_per_dev = recv_ref.shape[1]
    half = wet_ref.shape[0]
    cols = wet_ref.shape[2]
    quarters = cols // RUN
    halves = SUB // comps

    def copy_runs(to_grid, slot):
        def body(i, carry):
            for h in range(halves):
                for q in range(quarters):
                    s = inv_ref[(h * half + i) * quarters + q]
                    src = s // runs_per_dev
                    m = s % runs_per_dev
                    lanes = slice(q * RUN, (q + 1) * RUN)
                    rows = slice(h * comps, (h + 1) * comps)
                    if to_grid:
                        buf_ref[slot, i, rows, lanes] = recv_ref[src, m]
                    else:
                        out_ref[src, m] = buf_ref[slot, i, rows, lanes]
            return carry

        lax.fori_loop(0, half, body, 0)

    copy_runs(True, 0)
    ax = coef_ref[0]
    ay = coef_ref[1]
    south = coef_ref[2] > 0
    east = coef_ref[3] > 0
    cnt = coef_ref[4]
    sub_id = lax.broadcasted_iota(jnp.int32, (SUB, cols), 0)
    low = sub_id < comps
    for n in range(MAXSUB):
        src, dst = n % 2, (n + 1) % 2
        active = cnt > n
        sea = {}

        def sea_of(i):
            if i not in sea:
                sea[i] = buf_ref[src, i] * wet_ref[i]
            return sea[i]

        for i in range(half):
            if i == 0:
                prev = jnp.where(low, 0.0, pltpu.roll(sea_of(half - 1), comps, 0))
            else:
                prev = sea_of(i - 1)
            if i == half - 1:
                nxt = jnp.where(low, pltpu.roll(sea_of(0), comps, 0), 0.0)
            else:
                nxt = sea_of(i + 1)
            f = buf_ref[src, i]
            w = wet_ref[i]
            here = sea_of(i)
            up_row = jnp.where(south, prev, nxt)
            up_col = jnp.where(east, pltpu.roll(here, 1, 1), pltpu.roll(here, cols - 1, 1))
            moved = f - ax * (f - up_row) - ay * (f - up_col)
            buf_ref[dst, i] = jnp.where(active & (w > 0), moved, f)
            sea.pop(i - 1, None)
    copy_runs(False, MAXSUB % 2)


def propagate(inv, coef, recv, wet_h):
    half, _, cols = wet_h.shape
    smem = pl.BlockSpec(memory_space=pltpu.SMEM)
    vmem = pl.BlockSpec(memory_space=pltpu.VMEM)
    return pl.pallas_call(
        propagate_kernel,
        out_shape=jax.ShapeDtypeStruct(recv.shape, recv.dtype),
        in_specs=[smem] + [vmem] * 3,
        out_specs=vmem,
        scratch_shapes=[pltpu.VMEM((2, half, SUB, cols), jnp.float32)],
    )(inv, coef, recv, wet_h)


def on_device(spectrum, wind, growth, whitecap, courant, substeps, limiter, deck, wet):
    forced = sources(spectrum, wind, growth, whitecap, limiter)
    pt_count = lax.axis_size("pt")
    comp_count = lax.axis_size("comp")
    group_size = pt_count * comp_count
    total_comps = forced.shape[0]
    point_count = forced.shape[1]
    per_device = total_comps // group_size
    all_points = deck.shape[0]
    rows_grid = wet.shape[0]
    cols_grid = wet.shape[1]
    run_count = all_points // RUN
    runs_per_dev = point_count // RUN
    fields = lax.all_to_all(
        forced.reshape(group_size, per_device, runs_per_dev, RUN).transpose(0, 2, 1, 3),
        ("pt", "comp"),
        split_axis=0,
        concat_axis=0,
        tiled=True,
    )
    own_rank = lax.axis_index("pt") * comp_count + lax.axis_index("comp")
    comps = own_rank * per_device + jnp.arange(per_device, dtype=jnp.int32)
    angle = 2.0 * math.pi / DIRS * ((comps % DIRS).astype(jnp.float32) + 0.5)
    speed = courant[comps // DIRS]
    cross = speed * jnp.sin(angle)
    along = speed * jnp.cos(angle)
    counts = substeps[comps]
    halves = SUB // per_device
    half = rows_grid // halves
    lane_rows = jnp.stack([jnp.abs(cross), jnp.abs(along), (cross > 0).astype(jnp.float32),
                           (along > 0).astype(jnp.float32), counts.astype(jnp.float32)])
    coef = jnp.broadcast_to(jnp.tile(lane_rows, (1, halves))[:, :, None], (5, SUB, cols_grid))
    wet_h = jnp.broadcast_to(
        wet.astype(jnp.float32).reshape(halves, 1, half, cols_grid), (halves, per_device, half, cols_grid)
    ).reshape(SUB, half, cols_grid).transpose(1, 0, 2)
    slot_runs = deck.reshape(run_count, RUN)[:, 0] // RUN
    run_ids = jnp.arange(run_count, dtype=jnp.int32)
    inv = jnp.sum(jnp.where(slot_runs[None, :] == run_ids[:, None], run_ids[None, :], 0), axis=1)
    slots = propagate(inv, coef, fields, wet_h)
    back = lax.all_to_all(slots, ("pt", "comp"), split_axis=0, concat_axis=0, tiled=True)
    arrived = back.transpose(0, 2, 1, 3).reshape(total_comps, point_count)
    height = 4.0 * jnp.sqrt(jnp.mean(arrived, axis=0) + 1e-06)
    return (arrived, height)


def solution(mesh):
    in_specs = (
        P(None, ("pt", "comp")),
        P(("pt", "comp")),
        P(),
        P(),
        P(),
        P(),
        P(("pt", "comp")),
        P(),
        P(),
    )
    out_specs = (P(None, ("pt", "comp")), P(("pt", "comp")))
    return jax.shard_map(
        on_device, mesh=mesh, in_specs=in_specs, out_specs=out_specs, check_vma=False
    )
```

```python
import functools
import math

import jax
import jax.numpy as jnp
from jax import lax
from jax.experimental import pallas as pl
from jax.experimental.pallas import tpu as pltpu
from jax.sharding import PartitionSpec as P

DIRS = 32
MAXSUB = 8
RUN = 128
SUB = 8


rate_limit = 0.5
time_step = 0.5


def sources(spectrum, wind, growth, whitecap, limiter):
    mean_energy = jnp.mean(spectrum, axis=0)
    rate = (
        wind[None, :] * growth[:, None]
        - whitecap[:, None] * (mean_energy / (1.0 + mean_energy))[None, :]
    )
    rate = jnp.where(limiter[None, :] == 1, rate_limit * jnp.tanh(rate / rate_limit), rate)
    return spectrum * jnp.exp(time_step * rate)


def propagate_kernel(inv_ref, coef_ref, recv_ref, wet_ref, out_ref, buf_ref):
    comps = recv_ref.shape[1]
    half = wet_ref.shape[0]
    cols = wet_ref.shape[2]
    quarters = cols // RUN
    halves = SUB // comps

    def copy_runs(to_grid, slot):
        def body(i, carry):
            for h in range(halves):
                for q in range(quarters):
                    s = inv_ref[(h * half + i) * quarters + q]
                    lanes = slice(q * RUN, (q + 1) * RUN)
                    rows = slice(h * comps, (h + 1) * comps)
                    if to_grid:
                        buf_ref[slot, i, rows, lanes] = recv_ref[s]
                    else:
                        out_ref[s] = buf_ref[slot, i, rows, lanes]
            return carry

        lax.fori_loop(0, half, body, 0)

    copy_runs(True, 0)
    ax = coef_ref[0]
    ay = coef_ref[1]
    south = coef_ref[2] > 0
    east = coef_ref[3] > 0
    cnt = coef_ref[4]
    sub_id = lax.broadcasted_iota(jnp.int32, (SUB, cols), 0)
    low = sub_id < comps
    for n in range(MAXSUB):
        src, dst = n % 2, (n + 1) % 2
        active = cnt > n
        sea = {}

        def sea_of(i):
            if i not in sea:
                sea[i] = buf_ref[src, i] * wet_ref[i]
            return sea[i]

        for i in range(half):
            if i == 0:
                prev = jnp.where(low, 0.0, pltpu.roll(sea_of(half - 1), comps, 0))
            else:
                prev = sea_of(i - 1)
            if i == half - 1:
                nxt = jnp.where(low, pltpu.roll(sea_of(0), comps, 0), 0.0)
            else:
                nxt = sea_of(i + 1)
            f = buf_ref[src, i]
            w = wet_ref[i]
            here = sea_of(i)
            up_row = jnp.where(south, prev, nxt)
            up_col = jnp.where(east, pltpu.roll(here, 1, 1), pltpu.roll(here, cols - 1, 1))
            moved = f - ax * (f - up_row) - ay * (f - up_col)
            buf_ref[dst, i] = jnp.where(active & (w > 0), moved, f)
            sea.pop(i - 1, None)
    copy_runs(False, MAXSUB % 2)


def propagate(inv, coef, recv, wet_h):
    half, _, cols = wet_h.shape
    smem = pl.BlockSpec(memory_space=pltpu.SMEM)
    vmem = pl.BlockSpec(memory_space=pltpu.VMEM)
    return pl.pallas_call(
        propagate_kernel,
        out_shape=jax.ShapeDtypeStruct(recv.shape, recv.dtype),
        in_specs=[smem] + [vmem] * 3,
        out_specs=vmem,
        scratch_shapes=[pltpu.VMEM((2, half, SUB, cols), jnp.float32)],
    )(inv, coef, recv, wet_h)


def on_device(spectrum, wind, growth, whitecap, courant, substeps, limiter, deck, wet):
    forced = sources(spectrum, wind, growth, whitecap, limiter)
    pt_count = lax.axis_size("pt")
    comp_count = lax.axis_size("comp")
    group_size = pt_count * comp_count
    total_comps = forced.shape[0]
    point_count = forced.shape[1]
    per_device = total_comps // group_size
    all_points = deck.shape[0]
    rows_grid = wet.shape[0]
    cols_grid = wet.shape[1]
    run_count = all_points // RUN
    runs_per_dev = point_count // RUN
    fields = lax.all_to_all(
        forced.reshape(group_size, per_device, runs_per_dev, RUN).transpose(0, 2, 1, 3),
        ("pt", "comp"),
        split_axis=0,
        concat_axis=0,
        tiled=True,
    )
    own_rank = lax.axis_index("pt") * comp_count + lax.axis_index("comp")
    comps = own_rank * per_device + jnp.arange(per_device, dtype=jnp.int32)
    angle = 2.0 * math.pi / DIRS * ((comps % DIRS).astype(jnp.float32) + 0.5)
    speed = courant[comps // DIRS]
    cross = speed * jnp.sin(angle)
    along = speed * jnp.cos(angle)
    counts = substeps[comps]
    halves = SUB // per_device
    half = rows_grid // halves
    lane_rows = jnp.stack([jnp.abs(cross), jnp.abs(along), (cross > 0).astype(jnp.float32),
                           (along > 0).astype(jnp.float32), counts.astype(jnp.float32)])
    coef = jnp.broadcast_to(jnp.tile(lane_rows, (1, halves))[:, :, None], (5, SUB, cols_grid))
    wet_h = jnp.broadcast_to(
        wet.astype(jnp.float32).reshape(halves, 1, half, cols_grid), (halves, per_device, half, cols_grid)
    ).reshape(SUB, half, cols_grid).transpose(1, 0, 2)
    slot_runs = deck.reshape(run_count, RUN)[:, 0] // RUN
    run_ids = jnp.arange(run_count, dtype=jnp.int32)
    inv = jnp.sum(jnp.where(slot_runs[None, :] == run_ids[:, None], run_ids[None, :], 0), axis=1)
    slots = propagate(inv, coef, fields.reshape(run_count, per_device, RUN), wet_h)
    slots = slots.reshape(fields.shape)
    back = lax.all_to_all(slots, ("pt", "comp"), split_axis=0, concat_axis=0, tiled=True)
    arrived = back.transpose(0, 2, 1, 3).reshape(total_comps, point_count)
    height = 4.0 * jnp.sqrt(jnp.mean(arrived, axis=0) + 1e-06)
    return (arrived, height)


def solution(mesh):
    in_specs = (
        P(None, ("pt", "comp")),
        P(("pt", "comp")),
        P(),
        P(),
        P(),
        P(),
        P(("pt", "comp")),
        P(),
        P(),
    )
    out_specs = (P(None, ("pt", "comp")), P(("pt", "comp")))
    return jax.shard_map(
        on_device, mesh=mesh, in_specs=in_specs, out_specs=out_specs, check_vma=False
    )
```

```python
import functools
import math

import jax
import jax.numpy as jnp
from jax import lax
from jax.experimental import pallas as pl
from jax.experimental.pallas import tpu as pltpu
from jax.sharding import PartitionSpec as P

DIRS = 32
MAXSUB = 8
CHUNKS = 2
RUN = 128
SUB = 8
CHUNKS = 2


rate_limit = 0.5
time_step = 0.5


def sources(spectrum, wind, growth, whitecap, limiter):
    mean_energy = jnp.mean(spectrum, axis=0)
    rate = (
        wind[None, :] * growth[:, None]
        - whitecap[:, None] * (mean_energy / (1.0 + mean_energy))[None, :]
    )
    rate = jnp.where(limiter[None, :] == 1, rate_limit * jnp.tanh(rate / rate_limit), rate)
    return spectrum * jnp.exp(time_step * rate)


def propagate_kernel(inv_ref, coef_ref, recv_ref, wet_ref, out_ref, buf_ref):
    comps = recv_ref.shape[1]
    half = wet_ref.shape[0]
    cols = wet_ref.shape[2]
    quarters = cols // RUN
    halves = SUB // comps

    def copy_runs(to_grid, slot):
        def body(i, carry):
            for h in range(halves):
                for q in range(quarters):
                    s = inv_ref[(h * half + i) * quarters + q]
                    lanes = slice(q * RUN, (q + 1) * RUN)
                    rows = slice(h * comps, (h + 1) * comps)
                    if to_grid:
                        buf_ref[slot, i, rows, lanes] = recv_ref[s]
                    else:
                        out_ref[s] = buf_ref[slot, i, rows, lanes]
            return carry

        lax.fori_loop(0, half, body, 0)

    copy_runs(True, 0)
    ax = coef_ref[0]
    ay = coef_ref[1]
    south = coef_ref[2] > 0
    east = coef_ref[3] > 0
    cnt = coef_ref[4]
    sub_id = lax.broadcasted_iota(jnp.int32, (SUB, cols), 0)
    low = sub_id < comps
    high = sub_id >= SUB - comps
    for n in range(MAXSUB):
        src, dst = n % 2, (n + 1) % 2
        active = cnt > n
        sea = {}

        def sea_of(i):
            if i not in sea:
                sea[i] = buf_ref[src, i] * wet_ref[i]
            return sea[i]

        for i in range(half):
            if i == 0:
                prev = jnp.where(low, 0.0, pltpu.roll(sea_of(half - 1), comps, 0))
            else:
                prev = sea_of(i - 1)
            if i == half - 1:
                nxt = jnp.where(high, 0.0, pltpu.roll(sea_of(0), SUB - comps, 0))
            else:
                nxt = sea_of(i + 1)
            f = buf_ref[src, i]
            w = wet_ref[i]
            here = sea_of(i)
            up_row = jnp.where(south, prev, nxt)
            up_col = jnp.where(east, pltpu.roll(here, 1, 1), pltpu.roll(here, cols - 1, 1))
            moved = f - ax * (f - up_row) - ay * (f - up_col)
            buf_ref[dst, i] = jnp.where(active & (w > 0), moved, f)
            sea.pop(i - 1, None)
    copy_runs(False, MAXSUB % 2)


def propagate(inv, coef, recv, wet_h):
    half, _, cols = wet_h.shape
    smem = pl.BlockSpec(memory_space=pltpu.SMEM)
    vmem = pl.BlockSpec(memory_space=pltpu.VMEM)
    return pl.pallas_call(
        propagate_kernel,
        out_shape=jax.ShapeDtypeStruct(recv.shape, recv.dtype),
        in_specs=[smem] + [vmem] * 3,
        out_specs=vmem,
        scratch_shapes=[pltpu.VMEM((2, half, SUB, cols), jnp.float32)],
    )(inv, coef, recv, wet_h)


def on_device(spectrum, wind, growth, whitecap, courant, substeps, limiter, deck, wet):
    forced = sources(spectrum, wind, growth, whitecap, limiter)
    pt_count = lax.axis_size("pt")
    comp_count = lax.axis_size("comp")
    group_size = pt_count * comp_count
    total_comps = forced.shape[0]
    point_count = forced.shape[1]
    per_device = total_comps // group_size
    all_points = deck.shape[0]
    rows_grid = wet.shape[0]
    cols_grid = wet.shape[1]
    run_count = all_points // RUN
    runs_per_dev = point_count // RUN
    chunk = per_device // CHUNKS
    own_rank = lax.axis_index("pt") * comp_count + lax.axis_index("comp")
    halves = SUB // chunk
    half = rows_grid // halves
    wet_h = jnp.broadcast_to(
        wet.astype(jnp.float32).reshape(halves, 1, half, cols_grid), (halves, chunk, half, cols_grid)
    ).reshape(SUB, half, cols_grid).transpose(1, 0, 2)
    slot_runs = deck.reshape(run_count, RUN)[:, 0] // RUN
    run_ids = jnp.arange(run_count, dtype=jnp.int32)
    inv = jnp.sum(jnp.where(slot_runs[None, :] == run_ids[:, None], run_ids[None, :], 0), axis=1)
    per_point = forced.reshape(group_size, per_device, runs_per_dev, RUN)
    results = []
    for part in range(CHUNKS):
        fields = lax.all_to_all(
            per_point[:, part * chunk:(part + 1) * chunk].transpose(0, 2, 1, 3),
            ("pt", "comp"),
            split_axis=0,
            concat_axis=0,
            tiled=True,
        )
        comps = own_rank * per_device + part * chunk + jnp.arange(chunk, dtype=jnp.int32)
        angle = 2.0 * math.pi / DIRS * ((comps % DIRS).astype(jnp.float32) + 0.5)
        speed = courant[comps // DIRS]
        cross = speed * jnp.sin(angle)
        along = speed * jnp.cos(angle)
        counts = substeps[comps]
        lane_rows = jnp.stack([jnp.abs(cross), jnp.abs(along), (cross > 0).astype(jnp.float32),
                               (along > 0).astype(jnp.float32), counts.astype(jnp.float32)])
        coef = jnp.broadcast_to(jnp.tile(lane_rows, (1, halves))[:, :, None], (5, SUB, cols_grid))
        slots = propagate(inv, coef, fields.reshape(run_count, chunk, RUN), wet_h)
        results.append(lax.all_to_all(slots.reshape(fields.shape), ("pt", "comp"), split_axis=0, concat_axis=0, tiled=True))
    back = jnp.concatenate(results, axis=2)
    arrived = back.transpose(0, 2, 1, 3).reshape(total_comps, point_count)
    height = 4.0 * jnp.sqrt(jnp.mean(arrived, axis=0) + 1e-06)
    return (arrived, height)


def solution(mesh):
    in_specs = (
        P(None, ("pt", "comp")),
        P(("pt", "comp")),
        P(),
        P(),
        P(),
        P(),
        P(("pt", "comp")),
        P(),
        P(),
    )
    out_specs = (P(None, ("pt", "comp")), P(("pt", "comp")))
    return jax.shard_map(
        on_device, mesh=mesh, in_specs=in_specs, out_specs=out_specs, check_vma=False
    )
```

```python
import functools
import math

import jax
import jax.numpy as jnp
from jax import lax
from jax.experimental import pallas as pl
from jax.experimental.pallas import tpu as pltpu
from jax.sharding import PartitionSpec as P

DIRS = 32
MAXSUB = 8
RUN = 128
SUB = 8


rate_limit = 0.5
time_step = 0.5


def sources(spectrum, wind, growth, whitecap, limiter):
    mean_energy = jnp.mean(spectrum, axis=0)
    rate = (
        wind[None, :] * growth[:, None]
        - whitecap[:, None] * (mean_energy / (1.0 + mean_energy))[None, :]
    )
    rate = jnp.where(limiter[None, :] == 1, rate_limit * jnp.tanh(rate / rate_limit), rate)
    return spectrum * jnp.exp(time_step * rate)


def propagate_kernel(inv_ref, coef_ref, recv_ref, wet_ref, out_ref, buf_ref):
    comps = recv_ref.shape[1]
    half = wet_ref.shape[0]
    cols = wet_ref.shape[2]
    quarters = cols // RUN
    halves = SUB // comps

    def copy_runs(to_grid, slot):
        def body(i, carry):
            for h in range(halves):
                for q in range(quarters):
                    s = inv_ref[(h * half + i) * quarters + q]
                    lanes = slice(q * RUN, (q + 1) * RUN)
                    rows = slice(h * comps, (h + 1) * comps)
                    if to_grid:
                        buf_ref[slot, i, rows, lanes] = recv_ref[s]
                    else:
                        out_ref[s] = buf_ref[slot, i, rows, lanes]
            return carry

        lax.fori_loop(0, half, body, 0)

    copy_runs(True, 0)
    ax_all = coef_ref[0]
    ay_all = coef_ref[1]
    south = coef_ref[2] > 0
    east = coef_ref[3] > 0
    cnt = coef_ref[4]
    sub_id = lax.broadcasted_iota(jnp.int32, (SUB, cols), 0)
    low = sub_id < comps
    for n in range(MAXSUB):
        src, dst = n % 2, (n + 1) % 2
        active = cnt > n
        ax = jnp.where(active, ax_all, 0.0)
        ay = jnp.where(active, ay_all, 0.0)
        keep = 1.0 - ax - ay
        sea = {}

        def sea_of(i):
            if i not in sea:
                sea[i] = buf_ref[src, i] * wet_ref[i]
            return sea[i]

        for i in range(half):
            if i == 0:
                prev = jnp.where(low, 0.0, pltpu.roll(sea_of(half - 1), comps, 0))
            else:
                prev = sea_of(i - 1)
            if i == half - 1:
                nxt = jnp.where(low, pltpu.roll(sea_of(0), comps, 0), 0.0)
            else:
                nxt = sea_of(i + 1)
            f = buf_ref[src, i]
            w = wet_ref[i]
            here = sea_of(i)
            up_row = jnp.where(south, prev, nxt)
            up_col = jnp.where(east, pltpu.roll(here, 1, 1), pltpu.roll(here, cols - 1, 1))
            moved = keep * f + ax * up_row + ay * up_col
            buf_ref[dst, i] = jnp.where(w > 0, moved, f)
            sea.pop(i - 1, None)
    copy_runs(False, MAXSUB % 2)


def propagate(inv, coef, recv, wet_h):
    half, _, cols = wet_h.shape
    smem = pl.BlockSpec(memory_space=pltpu.SMEM)
    vmem = pl.BlockSpec(memory_space=pltpu.VMEM)
    return pl.pallas_call(
        propagate_kernel,
        out_shape=jax.ShapeDtypeStruct(recv.shape, recv.dtype),
        in_specs=[smem] + [vmem] * 3,
        out_specs=vmem,
        scratch_shapes=[pltpu.VMEM((2, half, SUB, cols), jnp.float32)],
    )(inv, coef, recv, wet_h)


def on_device(spectrum, wind, growth, whitecap, courant, substeps, limiter, deck, wet):
    pt_count = lax.axis_size("pt")
    comp_count = lax.axis_size("comp")
    group_size = pt_count * comp_count
    total_comps = spectrum.shape[0]
    point_count = spectrum.shape[1]
    per_device = total_comps // group_size
    all_points = deck.shape[0]
    rows_grid = wet.shape[0]
    cols_grid = wet.shape[1]
    run_count = all_points // RUN
    runs_per_dev = point_count // RUN
    mean_energy = jnp.mean(spectrum, axis=0).reshape(runs_per_dev, 1, RUN)
    ordered = spectrum.reshape(group_size, per_device, runs_per_dev, RUN).transpose(0, 2, 1, 3)
    rate = (
        wind.reshape(runs_per_dev, 1, RUN) * growth.reshape(group_size, 1, per_device, 1)
        - whitecap.reshape(group_size, 1, per_device, 1) * (mean_energy / (1.0 + mean_energy))
    )
    rate = jnp.where(limiter.reshape(runs_per_dev, 1, RUN) == 1, rate_limit * jnp.tanh(rate / rate_limit), rate)
    forced = ordered * jnp.exp(time_step * rate)
    fields = lax.all_to_all(
        forced,
        ("pt", "comp"),
        split_axis=0,
        concat_axis=0,
        tiled=True,
    )
    own_rank = lax.axis_index("pt") * comp_count + lax.axis_index("comp")
    comps = own_rank * per_device + jnp.arange(per_device, dtype=jnp.int32)
    angle = 2.0 * math.pi / DIRS * ((comps % DIRS).astype(jnp.float32) + 0.5)
    speed = courant[comps // DIRS]
    cross = speed * jnp.sin(angle)
    along = speed * jnp.cos(angle)
    counts = substeps[comps]
    halves = SUB // per_device
    half = rows_grid // halves
    lane_rows = jnp.stack([jnp.abs(cross), jnp.abs(along), (cross > 0).astype(jnp.float32),
                           (along > 0).astype(jnp.float32), counts.astype(jnp.float32)])
    coef = jnp.broadcast_to(jnp.tile(lane_rows, (1, halves))[:, :, None], (5, SUB, cols_grid))
    wet_h = jnp.broadcast_to(
        wet.astype(jnp.float32).reshape(halves, 1, half, cols_grid), (halves, per_device, half, cols_grid)
    ).reshape(SUB, half, cols_grid).transpose(1, 0, 2)
    slot_runs = deck.reshape(run_count, RUN)[:, 0] // RUN
    run_ids = jnp.arange(run_count, dtype=jnp.int32)
    inv = jnp.sum(jnp.where(slot_runs[None, :] == run_ids[:, None], run_ids[None, :], 0), axis=1)
    slots = propagate(inv, coef, fields.reshape(run_count, per_device, RUN), wet_h)
    slots = slots.reshape(fields.shape)
    back = lax.all_to_all(slots, ("pt", "comp"), split_axis=0, concat_axis=0, tiled=True)
    arrived = back.transpose(0, 2, 1, 3).reshape(total_comps, point_count)
    height = 4.0 * jnp.sqrt(jnp.mean(arrived, axis=0) + 1e-06)
    return (arrived, height)


def solution(mesh):
    in_specs = (
        P(None, ("pt", "comp")),
        P(("pt", "comp")),
        P(),
        P(),
        P(),
        P(),
        P(("pt", "comp")),
        P(),
        P(),
    )
    out_specs = (P(None, ("pt", "comp")), P(("pt", "comp")))
    return jax.shard_map(
        on_device, mesh=mesh, in_specs=in_specs, out_specs=out_specs, check_vma=False
    )
```

```python
import functools
import math

import jax
import jax.numpy as jnp
from jax import lax
from jax.experimental import pallas as pl
from jax.experimental.pallas import tpu as pltpu
from jax.sharding import PartitionSpec as P

DIRS = 32
MAXSUB = 8
RUN = 128
SUB = 8


rate_limit = 0.5
time_step = 0.5


def sources(spectrum, wind, growth, whitecap, limiter):
    mean_energy = jnp.mean(spectrum, axis=0)
    rate = (
        wind[None, :] * growth[:, None]
        - whitecap[:, None] * (mean_energy / (1.0 + mean_energy))[None, :]
    )
    rate = jnp.where(limiter[None, :] == 1, rate_limit * jnp.tanh(rate / rate_limit), rate)
    return spectrum * jnp.exp(time_step * rate)


def propagate_kernel(inv_ref, shift_ref, coef_ref, recv_ref, wet_ref, out_ref, buf_ref):
    comps = recv_ref.shape[1]
    half = wet_ref.shape[0]
    cols = wet_ref.shape[2]
    quarters = cols // RUN
    halves = SUB // comps

    def copy_runs(to_grid, slot):
        def body(i, carry):
            for h in range(halves):
                for q in range(quarters):
                    s = inv_ref[(h * half + i) * quarters + q]
                    lanes = slice(q * RUN, (q + 1) * RUN)
                    rows = slice(h * comps, (h + 1) * comps)
                    if to_grid:
                        buf_ref[slot, i, rows, lanes] = recv_ref[s]
                    else:
                        out_ref[s] = buf_ref[slot, i, rows, lanes]
            return carry

        lax.fori_loop(0, half, body, 0, unroll=8)

    copy_runs(True, 0)
    ax = coef_ref[0]
    ay = coef_ref[1]
    south = coef_ref[2] > 0
    shift = shift_ref[0]
    cnt = coef_ref[4]
    sub_id = lax.broadcasted_iota(jnp.int32, (SUB, cols), 0)
    low = sub_id < comps
    for n in range(MAXSUB):
        src, dst = n % 2, (n + 1) % 2
        active = cnt > n
        sea = {}
        vals = {}

        def sea_of(i):
            if i not in sea:
                vals[i] = (buf_ref[src, i], wet_ref[i])
                sea[i] = vals[i][0] * vals[i][1]
            return sea[i]

        for i in range(half):
            if i == 0:
                prev = jnp.where(low, 0.0, pltpu.roll(sea_of(half - 1), comps, 0))
            else:
                prev = sea_of(i - 1)
            if i == half - 1:
                nxt = jnp.where(low, pltpu.roll(sea_of(0), comps, 0), 0.0)
            else:
                nxt = sea_of(i + 1)
            here = sea_of(i)
            f, w = vals[i]
            up_row = jnp.where(south, prev, nxt)
            up_col = pltpu.roll(here, shift, 1)
            moved = f - ax * (f - up_row) - ay * (f - up_col)
            buf_ref[dst, i] = jnp.where(active & (w > 0), moved, f)
            sea.pop(i - 1, None)
            vals.pop(i - 1, None)
    copy_runs(False, MAXSUB % 2)


def propagate(inv, shift, coef, recv, wet_h):
    half, _, cols = wet_h.shape
    smem = pl.BlockSpec(memory_space=pltpu.SMEM)
    vmem = pl.BlockSpec(memory_space=pltpu.VMEM)
    return pl.pallas_call(
        propagate_kernel,
        out_shape=jax.ShapeDtypeStruct(recv.shape, recv.dtype),
        in_specs=[smem] * 2 + [vmem] * 3,
        out_specs=vmem,
        scratch_shapes=[pltpu.VMEM((2, half, SUB, cols), jnp.float32)],
    )(inv, shift, coef, recv, wet_h)


def on_device(spectrum, wind, growth, whitecap, courant, substeps, limiter, deck, wet):
    forced = sources(spectrum, wind, growth, whitecap, limiter)
    pt_count = lax.axis_size("pt")
    comp_count = lax.axis_size("comp")
    group_size = pt_count * comp_count
    total_comps = forced.shape[0]
    point_count = forced.shape[1]
    per_device = total_comps // group_size
    all_points = deck.shape[0]
    rows_grid = wet.shape[0]
    cols_grid = wet.shape[1]
    run_count = all_points // RUN
    runs_per_dev = point_count // RUN
    fields = lax.all_to_all(
        forced.reshape(group_size, per_device, runs_per_dev, RUN).transpose(0, 2, 1, 3),
        ("pt", "comp"),
        split_axis=0,
        concat_axis=0,
        tiled=True,
    )
    own_rank = lax.axis_index("pt") * comp_count + lax.axis_index("comp")
    comps = own_rank * per_device + jnp.arange(per_device, dtype=jnp.int32)
    angle = 2.0 * math.pi / DIRS * ((comps % DIRS).astype(jnp.float32) + 0.5)
    speed = courant[comps // DIRS]
    cross = speed * jnp.sin(angle)
    along = speed * jnp.cos(angle)
    counts = substeps[comps]
    halves = SUB // per_device
    half = rows_grid // halves
    lane_rows = jnp.stack([jnp.abs(cross), jnp.abs(along), (cross > 0).astype(jnp.float32),
                           (along > 0).astype(jnp.float32), counts.astype(jnp.float32)])
    coef = jnp.broadcast_to(jnp.tile(lane_rows, (1, halves))[:, :, None], (5, SUB, cols_grid))
    wet_h = jnp.broadcast_to(
        wet.astype(jnp.float32).reshape(halves, 1, half, cols_grid), (halves, per_device, half, cols_grid)
    ).reshape(SUB, half, cols_grid).transpose(1, 0, 2)
    slot_runs = deck.reshape(run_count, RUN)[:, 0] // RUN
    run_ids = jnp.arange(run_count, dtype=jnp.int32)
    inv = jnp.sum(jnp.where(slot_runs[None, :] == run_ids[:, None], run_ids[None, :], 0), axis=1)
    shift = jnp.where(along[:1] > 0, 1, cols_grid - 1).astype(jnp.int32)
    slots = propagate(inv, shift, coef, fields.reshape(run_count, per_device, RUN), wet_h)
    slots = slots.reshape(fields.shape)
    back = lax.all_to_all(slots, ("pt", "comp"), split_axis=0, concat_axis=0, tiled=True)
    arrived = back.transpose(0, 2, 1, 3).reshape(total_comps, point_count)
    height = 4.0 * jnp.sqrt(jnp.mean(arrived, axis=0) + 1e-06)
    return (arrived, height)


def solution(mesh):
    in_specs = (
        P(None, ("pt", "comp")),
        P(("pt", "comp")),
        P(),
        P(),
        P(),
        P(),
        P(("pt", "comp")),
        P(),
        P(),
    )
    out_specs = (P(None, ("pt", "comp")), P(("pt", "comp")))
    return jax.shard_map(
        on_device, mesh=mesh, in_specs=in_specs, out_specs=out_specs, check_vma=False
    )
```

```python
import functools
import math

import jax
import jax.numpy as jnp
from jax import lax
from jax.experimental import pallas as pl
from jax.experimental.pallas import tpu as pltpu
from jax.sharding import PartitionSpec as P

DIRS = 32
MAXSUB = 8
RUN = 128
SUB = 8


rate_limit = 0.5
time_step = 0.5


def sources(spectrum, wind, growth, whitecap, limiter):
    mean_energy = jnp.mean(spectrum, axis=0)
    rate = (
        wind[None, :] * growth[:, None]
        - whitecap[:, None] * (mean_energy / (1.0 + mean_energy))[None, :]
    )
    rate = jnp.where(limiter[None, :] == 1, rate_limit * jnp.tanh(rate / rate_limit), rate)
    return spectrum * jnp.exp(time_step * rate)


def propagate_kernel(inv_ref, shift_ref, coef_ref, recv_ref, wet_ref, out_ref, buf_ref):
    comps = recv_ref.shape[1]
    half = wet_ref.shape[0]
    cols = wet_ref.shape[2]
    quarters = cols // RUN
    halves = SUB // comps

    def copy_runs(to_grid, slot):
        def body(i, carry):
            for h in range(halves):
                for q in range(quarters):
                    s = inv_ref[(h * half + i) * quarters + q]
                    lanes = slice(q * RUN, (q + 1) * RUN)
                    rows = slice(h * comps, (h + 1) * comps)
                    if to_grid:
                        buf_ref[slot, i, rows, lanes] = recv_ref[s]
                    else:
                        out_ref[s] = buf_ref[slot, i, rows, lanes]
            return carry

        lax.fori_loop(0, half, body, 0, unroll=8)

    copy_runs(True, 0)
    ax = coef_ref[0]
    ay = coef_ref[1]
    south = coef_ref[2] > 0
    shift = shift_ref[0]
    cnt = coef_ref[4]
    sub_id = lax.broadcasted_iota(jnp.int32, (SUB, cols), 0)
    low = sub_id < comps
    for n in range(MAXSUB):
        src, dst = n % 2, (n + 1) % 2
        active = cnt > n
        sea = {}
        vals = {}

        def sea_of(i):
            if i not in sea:
                vals[i] = (buf_ref[src, i], wet_ref[i])
                sea[i] = vals[i][0] * vals[i][1]
            return sea[i]

        for i in range(half):
            if i == 0:
                prev = jnp.where(low, 0.0, pltpu.roll(sea_of(half - 1), comps, 0))
            else:
                prev = sea_of(i - 1)
            if i == half - 1:
                nxt = jnp.where(low, pltpu.roll(sea_of(0), comps, 0), 0.0)
            else:
                nxt = sea_of(i + 1)
            here = sea_of(i)
            f, w = vals[i]
            up_row = jnp.where(south, prev, nxt)
            up_col = pltpu.roll(here, shift, 1)
            moved = f - ax * (f - up_row) - ay * (f - up_col)
            result = jnp.where(active & (w > 0), moved, f)
            if n < MAXSUB - 1:
                buf_ref[dst, i] = result
            else:
                for h in range(halves):
                    for q in range(quarters):
                        out_ref[inv_ref[(h * half + i) * quarters + q]] = result[
                            h * comps:(h + 1) * comps, q * RUN:(q + 1) * RUN
                        ]
            sea.pop(i - 1, None)
            vals.pop(i - 1, None)


def propagate(inv, shift, coef, recv, wet_h):
    half, _, cols = wet_h.shape
    smem = pl.BlockSpec(memory_space=pltpu.SMEM)
    vmem = pl.BlockSpec(memory_space=pltpu.VMEM)
    return pl.pallas_call(
        propagate_kernel,
        out_shape=jax.ShapeDtypeStruct(recv.shape, recv.dtype),
        in_specs=[smem] * 2 + [vmem] * 3,
        out_specs=vmem,
        scratch_shapes=[pltpu.VMEM((2, half, SUB, cols), jnp.float32)],
    )(inv, shift, coef, recv, wet_h)


def on_device(spectrum, wind, growth, whitecap, courant, substeps, limiter, deck, wet):
    forced = sources(spectrum, wind, growth, whitecap, limiter)
    pt_count = lax.axis_size("pt")
    comp_count = lax.axis_size("comp")
    group_size = pt_count * comp_count
    total_comps = forced.shape[0]
    point_count = forced.shape[1]
    per_device = total_comps // group_size
    all_points = deck.shape[0]
    rows_grid = wet.shape[0]
    cols_grid = wet.shape[1]
    run_count = all_points // RUN
    runs_per_dev = point_count // RUN
    fields = lax.all_to_all(
        forced.reshape(group_size, per_device, runs_per_dev, RUN).transpose(0, 2, 1, 3),
        ("pt", "comp"),
        split_axis=0,
        concat_axis=0,
        tiled=True,
    )
    own_rank = lax.axis_index("pt") * comp_count + lax.axis_index("comp")
    comps = own_rank * per_device + jnp.arange(per_device, dtype=jnp.int32)
    angle = 2.0 * math.pi / DIRS * ((comps % DIRS).astype(jnp.float32) + 0.5)
    speed = courant[comps // DIRS]
    cross = speed * jnp.sin(angle)
    along = speed * jnp.cos(angle)
    counts = substeps[comps]
    halves = SUB // per_device
    half = rows_grid // halves
    lane_rows = jnp.stack([jnp.abs(cross), jnp.abs(along), (cross > 0).astype(jnp.float32),
                           (along > 0).astype(jnp.float32), counts.astype(jnp.float32)])
    coef = jnp.broadcast_to(jnp.tile(lane_rows, (1, halves))[:, :, None], (5, SUB, cols_grid))
    wet_h = jnp.broadcast_to(
        wet.astype(jnp.float32).reshape(halves, 1, half, cols_grid), (halves, per_device, half, cols_grid)
    ).reshape(SUB, half, cols_grid).transpose(1, 0, 2)
    slot_runs = deck.reshape(run_count, RUN)[:, 0] // RUN
    run_ids = jnp.arange(run_count, dtype=jnp.int32)
    inv = jnp.sum(jnp.where(slot_runs[None, :] == run_ids[:, None], run_ids[None, :], 0), axis=1)
    shift = jnp.where(along[:1] > 0, 1, cols_grid - 1).astype(jnp.int32)
    slots = propagate(inv, shift, coef, fields.reshape(run_count, per_device, RUN), wet_h)
    slots = slots.reshape(fields.shape)
    back = lax.all_to_all(slots, ("pt", "comp"), split_axis=0, concat_axis=0, tiled=True)
    arrived = back.transpose(0, 2, 1, 3).reshape(total_comps, point_count)
    height = 4.0 * jnp.sqrt(jnp.mean(arrived, axis=0) + 1e-06)
    return (arrived, height)


def solution(mesh):
    in_specs = (
        P(None, ("pt", "comp")),
        P(("pt", "comp")),
        P(),
        P(),
        P(),
        P(),
        P(("pt", "comp")),
        P(),
        P(),
    )
    out_specs = (P(None, ("pt", "comp")), P(("pt", "comp")))
    return jax.shard_map(
        on_device, mesh=mesh, in_specs=in_specs, out_specs=out_specs, check_vma=False
    )
```

```python
import functools
import math

import jax
import jax.numpy as jnp
from jax import lax
from jax.experimental import pallas as pl
from jax.experimental.pallas import tpu as pltpu
from jax.sharding import PartitionSpec as P

DIRS = 32
MAXSUB = 8
RUN = 128
SUB = 8


rate_limit = 0.5
time_step = 0.5


def sources(spectrum, wind, growth, whitecap, limiter):
    mean_energy = jnp.mean(spectrum, axis=0)
    rate = (
        wind[None, :] * growth[:, None]
        - whitecap[:, None] * (mean_energy / (1.0 + mean_energy))[None, :]
    )
    rate = jnp.where(limiter[None, :] == 1, rate_limit * jnp.tanh(rate / rate_limit), rate)
    return spectrum * jnp.exp(time_step * rate)


def propagate_kernel(inv_ref, shift_ref, coef_ref, recv_ref, wet_ref, out_ref, buf_ref):
    comps = recv_ref.shape[1]
    half = wet_ref.shape[0]
    cols = wet_ref.shape[2]
    quarters = cols // RUN
    halves = SUB // comps

    def copy_runs(to_grid, slot):
        def body(i, carry):
            for h in range(halves):
                for q in range(quarters):
                    s = inv_ref[(h * half + i) * quarters + q]
                    lanes = slice(q * RUN, (q + 1) * RUN)
                    rows = slice(h * comps, (h + 1) * comps)
                    if to_grid:
                        buf_ref[slot, i, rows, lanes] = recv_ref[s]
                    else:
                        out_ref[s] = buf_ref[slot, i, rows, lanes]
            return carry

        lax.fori_loop(0, half, body, 0, unroll=8)

    copy_runs(True, 0)
    shift = shift_ref[0]
    south = shift_ref[1] > 0
    sub_id = lax.broadcasted_iota(jnp.int32, (SUB, cols), 0)
    low = sub_id < comps
    sub_comp = jnp.where(low, sub_id, sub_id - comps)

    def per_sublane(row):
        v = jnp.full((SUB, cols), coef_ref[row * comps], jnp.float32)
        for c in range(1, comps):
            v = jnp.where(sub_comp == c, coef_ref[row * comps + c], v)
        return v

    ax = per_sublane(0)
    ay = per_sublane(1)
    cnt = per_sublane(2)
    for n in range(MAXSUB):
        src, dst = n % 2, (n + 1) % 2
        active = cnt > n
        sea = {}
        vals = {}

        def sea_of(i):
            if i not in sea:
                vals[i] = (buf_ref[src, i], wet_ref[i])
                sea[i] = vals[i][0] * vals[i][1]
            return sea[i]

        for i in range(half):
            if i == 0:
                prev = jnp.where(low, 0.0, pltpu.roll(sea_of(half - 1), comps, 0))
            else:
                prev = sea_of(i - 1)
            if i == half - 1:
                nxt = jnp.where(low, pltpu.roll(sea_of(0), comps, 0), 0.0)
            else:
                nxt = sea_of(i + 1)
            here = sea_of(i)
            f, w = vals[i]
            up_row = jnp.where(south, prev, nxt)
            up_col = pltpu.roll(here, shift, 1)
            moved = f - ax * (f - up_row) - ay * (f - up_col)
            result = jnp.where(active & (w > 0), moved, f)
            if n < MAXSUB - 1:
                buf_ref[dst, i] = result
            else:
                for h in range(halves):
                    for q in range(quarters):
                        out_ref[inv_ref[(h * half + i) * quarters + q]] = result[
                            h * comps:(h + 1) * comps, q * RUN:(q + 1) * RUN
                        ]
            sea.pop(i - 1, None)
            vals.pop(i - 1, None)


def propagate(inv, shift, coef, recv, wet_h):
    half, _, cols = wet_h.shape
    smem = pl.BlockSpec(memory_space=pltpu.SMEM)
    vmem = pl.BlockSpec(memory_space=pltpu.VMEM)
    return pl.pallas_call(
        propagate_kernel,
        out_shape=jax.ShapeDtypeStruct(recv.shape, recv.dtype),
        in_specs=[smem] * 3 + [vmem] * 2,
        out_specs=vmem,
        scratch_shapes=[pltpu.VMEM((2, half, SUB, cols), jnp.float32)],
    )(inv, shift, coef, recv, wet_h)


def on_device(spectrum, wind, growth, whitecap, courant, substeps, limiter, deck, wet):
    forced = sources(spectrum, wind, growth, whitecap, limiter)
    pt_count = lax.axis_size("pt")
    comp_count = lax.axis_size("comp")
    group_size = pt_count * comp_count
    total_comps = forced.shape[0]
    point_count = forced.shape[1]
    per_device = total_comps // group_size
    all_points = deck.shape[0]
    rows_grid = wet.shape[0]
    cols_grid = wet.shape[1]
    run_count = all_points // RUN
    runs_per_dev = point_count // RUN
    fields = lax.all_to_all(
        forced.reshape(group_size, per_device, runs_per_dev, RUN).transpose(0, 2, 1, 3),
        ("pt", "comp"),
        split_axis=0,
        concat_axis=0,
        tiled=True,
    )
    own_rank = lax.axis_index("pt") * comp_count + lax.axis_index("comp")
    comps = own_rank * per_device + jnp.arange(per_device, dtype=jnp.int32)
    angle = 2.0 * math.pi / DIRS * ((comps % DIRS).astype(jnp.float32) + 0.5)
    speed = courant[comps // DIRS]
    cross = speed * jnp.sin(angle)
    along = speed * jnp.cos(angle)
    counts = substeps[comps]
    halves = SUB // per_device
    half = rows_grid // halves
    coef = jnp.concatenate([jnp.abs(cross), jnp.abs(along), counts.astype(jnp.float32)])
    wet_h = jnp.broadcast_to(
        wet.astype(jnp.float32).reshape(halves, 1, half, cols_grid), (halves, per_device, half, cols_grid)
    ).reshape(SUB, half, cols_grid).transpose(1, 0, 2)
    slot_runs = deck.reshape(run_count, RUN)[:, 0] // RUN
    run_ids = jnp.arange(run_count, dtype=jnp.int32)
    inv = jnp.sum(jnp.where(slot_runs[None, :] == run_ids[:, None], run_ids[None, :], 0), axis=1)
    shift = jnp.stack([jnp.where(along[0] > 0, 1, cols_grid - 1), (cross[0] > 0).astype(jnp.int32)]).astype(jnp.int32)
    slots = propagate(inv, shift, coef, fields.reshape(run_count, per_device, RUN), wet_h)
    slots = slots.reshape(fields.shape)
    back = lax.all_to_all(slots, ("pt", "comp"), split_axis=0, concat_axis=0, tiled=True)
    arrived = back.transpose(0, 2, 1, 3).reshape(total_comps, point_count)
    height = 4.0 * jnp.sqrt(jnp.mean(arrived, axis=0) + 1e-06)
    return (arrived, height)


def solution(mesh):
    in_specs = (
        P(None, ("pt", "comp")),
        P(("pt", "comp")),
        P(),
        P(),
        P(),
        P(),
        P(("pt", "comp")),
        P(),
        P(),
    )
    out_specs = (P(None, ("pt", "comp")), P(("pt", "comp")))
    return jax.shard_map(
        on_device, mesh=mesh, in_specs=in_specs, out_specs=out_specs, check_vma=False
    )
```

```python
import functools
import math

import jax
import jax.numpy as jnp
from jax import lax
from jax.experimental import pallas as pl
from jax.experimental.pallas import tpu as pltpu
from jax.sharding import PartitionSpec as P

DIRS = 32
MAXSUB = 8
RUN = 128
SUB = 8


rate_limit = 0.5
time_step = 0.5


def sources(spectrum, wind, growth, whitecap, limiter):
    mean_energy = jnp.mean(spectrum, axis=0)
    rate = (
        wind[None, :] * growth[:, None]
        - whitecap[:, None] * (mean_energy / (1.0 + mean_energy))[None, :]
    )
    rate = jnp.where(limiter[None, :] == 1, rate_limit * jnp.tanh(rate / rate_limit), rate)
    return spectrum * jnp.exp(time_step * rate)


def propagate_kernel(inv_ref, shift_ref, coef_ref, recv_ref, wet_ref, out_ref, buf_ref):
    comps = recv_ref.shape[1]
    half = wet_ref.shape[0]
    cols = wet_ref.shape[2]
    quarters = cols // RUN
    halves = SUB // comps

    def copy_runs(to_grid, slot):
        def body(i, carry):
            for h in range(halves):
                for q in range(quarters):
                    s = inv_ref[(h * half + i) * quarters + q]
                    lanes = slice(q * RUN, (q + 1) * RUN)
                    rows = slice(h * comps, (h + 1) * comps)
                    if to_grid:
                        buf_ref[slot, i, rows, lanes] = recv_ref[s]
                    else:
                        out_ref[s] = buf_ref[slot, i, rows, lanes]
            return carry

        lax.fori_loop(0, half, body, 0, unroll=8)

    copy_runs(True, 0)
    shift = shift_ref[0]
    sub_id = lax.broadcasted_iota(jnp.int32, (SUB, cols), 0)
    low = sub_id < comps
    sub_comp = jnp.where(low, sub_id, sub_id - comps)

    def per_sublane(row):
        v = jnp.full((SUB, cols), coef_ref[row * comps], jnp.float32)
        for c in range(1, comps):
            v = jnp.where(sub_comp == c, coef_ref[row * comps + c], v)
        return v

    ax = per_sublane(0)
    ay = per_sublane(1)
    cnt = per_sublane(2)
    def run_substeps(south):
        for n in range(MAXSUB):
            src, dst = n % 2, (n + 1) % 2
            active = cnt > n
            sea = {}
            vals = {}

            def sea_of(i):
                if i not in sea:
                    vals[i] = (buf_ref[src, i], wet_ref[i])
                    sea[i] = vals[i][0] * vals[i][1]
                return sea[i]

            for i in range(half):
                if i == 0:
                    prev = jnp.where(low, 0.0, pltpu.roll(sea_of(half - 1), comps, 0))
                else:
                    prev = sea_of(i - 1)
                if i == half - 1:
                    nxt = jnp.where(low, pltpu.roll(sea_of(0), comps, 0), 0.0)
                else:
                    nxt = sea_of(i + 1)
                here = sea_of(i)
                f, w = vals[i]
                up_row = prev if south else nxt
                up_col = pltpu.roll(here, shift, 1)
                moved = f - ax * (f - up_row) - ay * (f - up_col)
                result = jnp.where(active & (w > 0), moved, f)
                if n < MAXSUB - 1:
                    buf_ref[dst, i] = result
                else:
                    for h in range(halves):
                        for q in range(quarters):
                            out_ref[inv_ref[(h * half + i) * quarters + q]] = result[
                                h * comps:(h + 1) * comps, q * RUN:(q + 1) * RUN
                            ]
                sea.pop(i - 1, None)
                vals.pop(i - 1, None)

    @pl.when(shift_ref[1] > 0)
    def _():
        run_substeps(True)

    @pl.when(shift_ref[1] <= 0)
    def _():
        run_substeps(False)


def propagate(inv, shift, coef, recv, wet_h):
    half, _, cols = wet_h.shape
    smem = pl.BlockSpec(memory_space=pltpu.SMEM)
    vmem = pl.BlockSpec(memory_space=pltpu.VMEM)
    return pl.pallas_call(
        propagate_kernel,
        out_shape=jax.ShapeDtypeStruct(recv.shape, recv.dtype),
        in_specs=[smem] * 3 + [vmem] * 2,
        out_specs=vmem,
        scratch_shapes=[pltpu.VMEM((2, half, SUB, cols), jnp.float32)],
    )(inv, shift, coef, recv, wet_h)


def on_device(spectrum, wind, growth, whitecap, courant, substeps, limiter, deck, wet):
    forced = sources(spectrum, wind, growth, whitecap, limiter)
    pt_count = lax.axis_size("pt")
    comp_count = lax.axis_size("comp")
    group_size = pt_count * comp_count
    total_comps = forced.shape[0]
    point_count = forced.shape[1]
    per_device = total_comps // group_size
    all_points = deck.shape[0]
    rows_grid = wet.shape[0]
    cols_grid = wet.shape[1]
    run_count = all_points // RUN
    runs_per_dev = point_count // RUN
    fields = lax.all_to_all(
        forced.reshape(group_size, per_device, runs_per_dev, RUN).transpose(0, 2, 1, 3),
        ("pt", "comp"),
        split_axis=0,
        concat_axis=0,
        tiled=True,
    )
    own_rank = lax.axis_index("pt") * comp_count + lax.axis_index("comp")
    comps = own_rank * per_device + jnp.arange(per_device, dtype=jnp.int32)
    angle = 2.0 * math.pi / DIRS * ((comps % DIRS).astype(jnp.float32) + 0.5)
    speed = courant[comps // DIRS]
    cross = speed * jnp.sin(angle)
    along = speed * jnp.cos(angle)
    counts = substeps[comps]
    halves = SUB // per_device
    half = rows_grid // halves
    coef = jnp.concatenate([jnp.abs(cross), jnp.abs(along), counts.astype(jnp.float32)])
    wet_h = jnp.broadcast_to(
        wet.astype(jnp.float32).reshape(halves, 1, half, cols_grid), (halves, per_device, half, cols_grid)
    ).reshape(SUB, half, cols_grid).transpose(1, 0, 2)
    slot_runs = deck.reshape(run_count, RUN)[:, 0] // RUN
    run_ids = jnp.arange(run_count, dtype=jnp.int32)
    inv = jnp.sum(jnp.where(slot_runs[None, :] == run_ids[:, None], run_ids[None, :], 0), axis=1)
    shift = jnp.stack([jnp.where(along[0] > 0, 1, cols_grid - 1), (cross[0] > 0).astype(jnp.int32)]).astype(jnp.int32)
    slots = propagate(inv, shift, coef, fields.reshape(run_count, per_device, RUN), wet_h)
    slots = slots.reshape(fields.shape)
    back = lax.all_to_all(slots, ("pt", "comp"), split_axis=0, concat_axis=0, tiled=True)
    arrived = back.transpose(0, 2, 1, 3).reshape(total_comps, point_count)
    height = 4.0 * jnp.sqrt(jnp.mean(arrived, axis=0) + 1e-06)
    return (arrived, height)


def solution(mesh):
    in_specs = (
        P(None, ("pt", "comp")),
        P(("pt", "comp")),
        P(),
        P(),
        P(),
        P(),
        P(("pt", "comp")),
        P(),
        P(),
    )
    out_specs = (P(None, ("pt", "comp")), P(("pt", "comp")))
    return jax.shard_map(
        on_device, mesh=mesh, in_specs=in_specs, out_specs=out_specs, check_vma=False
    )
```

```python
import functools
import math

import jax
import jax.numpy as jnp
from jax import lax
from jax.experimental import pallas as pl
from jax.experimental.pallas import tpu as pltpu
from jax.sharding import PartitionSpec as P

DIRS = 32
MAXSUB = 8
RUN = 128
SUB = 8


rate_limit = 0.5
time_step = 0.5


def sources(spectrum, wind, growth, whitecap, limiter):
    mean_energy = jnp.mean(spectrum, axis=0)
    rate = (
        wind[None, :] * growth[:, None]
        - whitecap[:, None] * (mean_energy / (1.0 + mean_energy))[None, :]
    )
    rate = jnp.where(limiter[None, :] == 1, rate_limit * jnp.tanh(rate / rate_limit), rate)
    return spectrum * jnp.exp(time_step * rate)


def propagate_kernel(inv_ref, shift_ref, coef_ref, recv_ref, wet_ref, out_ref, buf_ref):
    comps = recv_ref.shape[1]
    half = wet_ref.shape[0]
    cols = wet_ref.shape[2]
    quarters = cols // RUN
    halves = SUB // comps

    def copy_runs(to_grid, slot):
        def body(i, carry):
            for h in range(halves):
                for q in range(quarters):
                    s = inv_ref[(h * half + i) * quarters + q]
                    lanes = slice(q * RUN, (q + 1) * RUN)
                    rows = slice(h * comps, (h + 1) * comps)
                    if to_grid:
                        buf_ref[slot, i, rows, lanes] = recv_ref[s]
                    else:
                        out_ref[s] = buf_ref[slot, i, rows, lanes]
            return carry

        lax.fori_loop(0, half, body, 0, unroll=True)

    copy_runs(True, 0)
    shift = shift_ref[0]
    south = shift_ref[1] > 0
    sub_id = lax.broadcasted_iota(jnp.int32, (SUB, cols), 0)
    low = sub_id < comps
    sub_comp = jnp.where(low, sub_id, sub_id - comps)

    def per_sublane(row):
        v = jnp.full((SUB, cols), coef_ref[row * comps], jnp.float32)
        for c in range(1, comps):
            v = jnp.where(sub_comp == c, coef_ref[row * comps + c], v)
        return v

    ax = per_sublane(0)
    ay = per_sublane(1)
    cnt = per_sublane(2)
    for n in range(MAXSUB):
        src, dst = n % 2, (n + 1) % 2
        active = cnt > n
        sea = {}
        vals = {}

        def sea_of(i):
            if i not in sea:
                vals[i] = (buf_ref[src, i], wet_ref[i])
                sea[i] = vals[i][0] * vals[i][1]
            return sea[i]

        for i in range(half):
            if i == 0:
                prev = jnp.where(low, 0.0, pltpu.roll(sea_of(half - 1), comps, 0))
            else:
                prev = sea_of(i - 1)
            if i == half - 1:
                nxt = jnp.where(low, pltpu.roll(sea_of(0), comps, 0), 0.0)
            else:
                nxt = sea_of(i + 1)
            here = sea_of(i)
            f, w = vals[i]
            up_row = jnp.where(south, prev, nxt)
            up_col = pltpu.roll(here, shift, 1)
            moved = f - ax * (f - up_row) - ay * (f - up_col)
            result = jnp.where(active & (w > 0), moved, f)
            if n < MAXSUB - 1:
                buf_ref[dst, i] = result
            else:
                for h in range(halves):
                    for q in range(quarters):
                        out_ref[inv_ref[(h * half + i) * quarters + q]] = result[
                            h * comps:(h + 1) * comps, q * RUN:(q + 1) * RUN
                        ]
            sea.pop(i - 1, None)
            vals.pop(i - 1, None)


def propagate(inv, shift, coef, recv, wet_h):
    half, _, cols = wet_h.shape
    smem = pl.BlockSpec(memory_space=pltpu.SMEM)
    vmem = pl.BlockSpec(memory_space=pltpu.VMEM)
    return pl.pallas_call(
        propagate_kernel,
        out_shape=jax.ShapeDtypeStruct(recv.shape, recv.dtype),
        in_specs=[smem] * 3 + [vmem] * 2,
        out_specs=vmem,
        scratch_shapes=[pltpu.VMEM((2, half, SUB, cols), jnp.float32)],
    )(inv, shift, coef, recv, wet_h)


def on_device(spectrum, wind, growth, whitecap, courant, substeps, limiter, deck, wet):
    forced = sources(spectrum, wind, growth, whitecap, limiter)
    pt_count = lax.axis_size("pt")
    comp_count = lax.axis_size("comp")
    group_size = pt_count * comp_count
    total_comps = forced.shape[0]
    point_count = forced.shape[1]
    per_device = total_comps // group_size
    all_points = deck.shape[0]
    rows_grid = wet.shape[0]
    cols_grid = wet.shape[1]
    run_count = all_points // RUN
    runs_per_dev = point_count // RUN
    fields = lax.all_to_all(
        forced.reshape(group_size, per_device, runs_per_dev, RUN).transpose(0, 2, 1, 3),
        ("pt", "comp"),
        split_axis=0,
        concat_axis=0,
        tiled=True,
    )
    own_rank = lax.axis_index("pt") * comp_count + lax.axis_index("comp")
    comps = own_rank * per_device + jnp.arange(per_device, dtype=jnp.int32)
    angle = 2.0 * math.pi / DIRS * ((comps % DIRS).astype(jnp.float32) + 0.5)
    speed = courant[comps // DIRS]
    cross = speed * jnp.sin(angle)
    along = speed * jnp.cos(angle)
    counts = substeps[comps]
    halves = SUB // per_device
    half = rows_grid // halves
    coef = jnp.concatenate([jnp.abs(cross), jnp.abs(along), counts.astype(jnp.float32)])
    wet_h = jnp.broadcast_to(
        wet.astype(jnp.float32).reshape(halves, 1, half, cols_grid), (halves, per_device, half, cols_grid)
    ).reshape(SUB, half, cols_grid).transpose(1, 0, 2)
    slot_runs = deck.reshape(run_count, RUN)[:, 0] // RUN
    run_ids = jnp.arange(run_count, dtype=jnp.int32)
    inv = jnp.sum(jnp.where(slot_runs[None, :] == run_ids[:, None], run_ids[None, :], 0), axis=1)
    shift = jnp.stack([jnp.where(along[0] > 0, 1, cols_grid - 1), (cross[0] > 0).astype(jnp.int32)]).astype(jnp.int32)
    slots = propagate(inv, shift, coef, fields.reshape(run_count, per_device, RUN), wet_h)
    slots = slots.reshape(fields.shape)
    back = lax.all_to_all(slots, ("pt", "comp"), split_axis=0, concat_axis=0, tiled=True)
    arrived = back.transpose(0, 2, 1, 3).reshape(total_comps, point_count)
    height = 4.0 * jnp.sqrt(jnp.mean(arrived, axis=0) + 1e-06)
    return (arrived, height)


def solution(mesh):
    in_specs = (
        P(None, ("pt", "comp")),
        P(("pt", "comp")),
        P(),
        P(),
        P(),
        P(),
        P(("pt", "comp")),
        P(),
        P(),
    )
    out_specs = (P(None, ("pt", "comp")), P(("pt", "comp")))
    return jax.shard_map(
        on_device, mesh=mesh, in_specs=in_specs, out_specs=out_specs, check_vma=False
    )
```

```python
import functools
import math

import jax
import jax.numpy as jnp
from jax import lax
from jax.experimental import pallas as pl
from jax.experimental.pallas import tpu as pltpu
from jax.sharding import PartitionSpec as P

DIRS = 32
MAXSUB = 8
RUN = 128
SUB = 8


rate_limit = 0.5
time_step = 0.5


def sources(spectrum, wind, growth, whitecap, limiter):
    mean_energy = jnp.mean(spectrum, axis=0)
    rate = (
        wind[None, :] * growth[:, None]
        - whitecap[:, None] * (mean_energy / (1.0 + mean_energy))[None, :]
    )
    rate = jnp.where(limiter[None, :] == 1, rate_limit * jnp.tanh(rate / rate_limit), rate)
    return spectrum * jnp.exp(time_step * rate)


def propagate_kernel(inv_ref, shift_ref, coef_ref, recv_ref, wet_ref, out_ref, buf_ref):
    comps = recv_ref.shape[1]
    half = wet_ref.shape[0]
    cols = wet_ref.shape[2]
    quarters = cols // RUN
    halves = SUB // comps

    def copy_runs(to_grid, slot):
        def body(i, carry):
            for h in range(halves):
                for q in range(quarters):
                    s = inv_ref[(h * half + i) * quarters + q]
                    lanes = slice(q * RUN, (q + 1) * RUN)
                    rows = slice(h * comps, (h + 1) * comps)
                    if to_grid:
                        buf_ref[slot, i, rows, lanes] = recv_ref[s]
                    else:
                        out_ref[s] = buf_ref[slot, i, rows, lanes]
            return carry

        lax.fori_loop(0, half, body, 0, unroll=True)

    copy_runs(True, 0)
    shift = shift_ref[0]
    south = shift_ref[1] > 0
    sub_id = lax.broadcasted_iota(jnp.int32, (SUB, cols), 0)
    low = sub_id < comps
    sub_comp = jnp.where(low, sub_id, sub_id - comps)

    def per_sublane(row):
        v = jnp.full((SUB, cols), coef_ref[row * comps], jnp.float32)
        for c in range(1, comps):
            v = jnp.where(sub_comp == c, coef_ref[row * comps + c], v)
        return v

    ax = per_sublane(0)
    ay = per_sublane(1)
    cnt = per_sublane(2)
    for n in range(MAXSUB):
        src, dst = n % 2, (n + 1) % 2
        active = cnt > n
        sea = {}
        vals = {}

        def sea_of(i):
            if i not in sea:
                vals[i] = (buf_ref[src, i], wet_ref[i])
                sea[i] = vals[i][0] * vals[i][1]
            return sea[i]

        for i in range(half):
            if i == 0:
                prev = jnp.where(low, 0.0, pltpu.roll(sea_of(half - 1), comps, 0))
            else:
                prev = sea_of(i - 1)
            if i == half - 1:
                nxt = jnp.where(low, pltpu.roll(sea_of(0), comps, 0), 0.0)
            else:
                nxt = sea_of(i + 1)
            here = sea_of(i)
            f, w = vals[i]
            up_row = jnp.where(south, prev, nxt)
            up_col = pltpu.roll(here, shift, 1)
            moved = f - ax * (f - up_row) - ay * (f - up_col)
            result = jnp.where(active & (w > 0), moved, f)
            if n < MAXSUB - 1:
                buf_ref[dst, i] = result
            else:
                for h in range(halves):
                    for q in range(quarters):
                        out_ref[inv_ref[(h * half + i) * quarters + q]] = result[
                            h * comps:(h + 1) * comps, q * RUN:(q + 1) * RUN
                        ]
            sea.pop(i - 1, None)
            vals.pop(i - 1, None)


def propagate(inv, shift, coef, recv, wet_h):
    half, _, cols = wet_h.shape
    smem = pl.BlockSpec(memory_space=pltpu.SMEM)
    vmem = pl.BlockSpec(memory_space=pltpu.VMEM)
    return pl.pallas_call(
        propagate_kernel,
        out_shape=jax.ShapeDtypeStruct(recv.shape, recv.dtype),
        in_specs=[smem] * 3 + [vmem] * 2,
        out_specs=vmem,
        scratch_shapes=[pltpu.VMEM((2, half, SUB, cols), jnp.float32)],
    )(inv, shift, coef, recv, wet_h)


def on_device(spectrum, wind, growth, whitecap, courant, substeps, limiter, deck, wet):
    forced = sources(spectrum, wind, growth, whitecap, limiter)
    pt_count = lax.axis_size("pt")
    comp_count = lax.axis_size("comp")
    group_size = pt_count * comp_count
    total_comps = forced.shape[0]
    point_count = forced.shape[1]
    per_device = total_comps // group_size
    all_points = deck.shape[0]
    rows_grid = wet.shape[0]
    cols_grid = wet.shape[1]
    run_count = all_points // RUN
    runs_per_dev = point_count // RUN
    fields = lax.all_to_all(
        forced.reshape(group_size, per_device, runs_per_dev, RUN).transpose(0, 2, 1, 3),
        ("pt", "comp"),
        split_axis=0,
        concat_axis=0,
        tiled=True,
    )
    own_rank = lax.axis_index("pt") * comp_count + lax.axis_index("comp")
    comps = own_rank * per_device + jnp.arange(per_device, dtype=jnp.int32)
    angle = 2.0 * math.pi / DIRS * ((comps % DIRS).astype(jnp.float32) + 0.5)
    speed = courant[comps // DIRS]
    cross = speed * jnp.sin(angle)
    along = speed * jnp.cos(angle)
    counts = substeps[comps]
    halves = SUB // per_device
    half = rows_grid // halves
    coef = jnp.concatenate([jnp.abs(cross), jnp.abs(along), counts.astype(jnp.float32)])
    wet_h = jnp.broadcast_to(
        wet.astype(jnp.float32).reshape(halves, 1, half, cols_grid), (halves, per_device, half, cols_grid)
    ).reshape(SUB, half, cols_grid).transpose(1, 0, 2)
    slot_runs = deck.reshape(run_count, RUN)[:, 0] // RUN
    run_ids = jnp.arange(run_count, dtype=jnp.int32)
    inv = jnp.sum(jnp.where(slot_runs[None, :] == run_ids[:, None], run_ids[None, :], 0), axis=1)
    shift = jnp.stack([jnp.where(along[0] > 0, 1, cols_grid - 1), (cross[0] > 0).astype(jnp.int32)]).astype(jnp.int32)
    slots = propagate(inv, shift, coef, fields.reshape(run_count, per_device, RUN), wet_h)
    slots = slots.reshape(fields.shape)
    back = lax.all_to_all(slots, ("pt", "comp"), split_axis=0, concat_axis=0, tiled=True)
    arrived = back.transpose(0, 2, 1, 3).reshape(total_comps, point_count)
    height = 4.0 * jnp.sqrt(jnp.sum(back, axis=(0, 2)).reshape(point_count) / total_comps + 1e-06)
    return (arrived, height)


def solution(mesh):
    in_specs = (
        P(None, ("pt", "comp")),
        P(("pt", "comp")),
        P(),
        P(),
        P(),
        P(),
        P(("pt", "comp")),
        P(),
        P(),
    )
    out_specs = (P(None, ("pt", "comp")), P(("pt", "comp")))
    return jax.shard_map(
        on_device, mesh=mesh, in_specs=in_specs, out_specs=out_specs, check_vma=False
    )
```
